32 devices in a mesh: gx: 4 (over z), gy: 2 (over y), gz: 4 (over x, core).
Axes of the slice: x: 2, y: 2, z: 4, core: 2. Of those that a mesh axis runs over, the one named last changes fastest.
Arguments:
- adjoint_guess: float32 [2, 20, 128, 1024], P(None, 'gz', 'gy', 'gx'), may hold values from -6 to 6
- viscosity: float32 [20, 128, 1024], P('gz', 'gy', 'gx'), may hold values from 0.2 to 2
- friction: float32 [128, 1024], P('gy', 'gx'), may hold values from 0.2 to 5
- base_velocity: float32 [2, 128, 1024], P(None, 'gy', 'gx'), may hold values from -6 to 6
- surface_slope: float32 [2, 128, 1024], P(None, 'gy', 'gx'), may hold values from -6 to 6
- ice_mask: int32 [128, 1024], P('gy', 'gx'), may hold values 0 or 1
- pixel_misfit: float32 [524288], P(('gx', 'gy', 'gz')), may hold values from -6 to 6
- pixel_look: float32 [524288], P(('gx', 'gy', 'gz')), may hold values from -3.140625 to 3.140625
- pixel_tile: int32 [524288, 1], P(('gx', 'gy', 'gz')), may hold values from 0 to 7; in each aligned block of 16384 rows (0 to 16383, 16384 to 32767, ...) at most 4096 rows name the same one
- pixel_cell: int32 [524288], P(('gx', 'gy', 'gz')), may hold values from 0 to 16383
- pixel_count: int32 [32], P(('gx', 'gy', 'gz')), may hold values from 1 to 16384, 393216 in all
Outputs:
- adjoint: float32 [2, 20, 128, 1024], P(None, 'gz', 'gy', 'gx')
- sensitivity_maps: float32 [2, 128, 1024], P(None, ('gy', 'gz'), 'gx')
The draws below stay inside these ranges and needn't reach their ends.
Inputs may be any that keep to these rules, and one draw needn't show every extreme that they name: `pixel_tile`: among the rows of one device no tile is named more than 4096 times, a bound that some block reaches. `pixel_count`: rows of a device from its count on are padding.
All inputs are finite; a program needn't handle non-finite values. No bound on the sum of `ice_mask` on one device may be relied on, other than what follows from the above.
Results may differ from the reference program's by a relative error of at most 0.00002.
Values sent between devices are 32-bit elements; how exact they have to be, the bound alone decides.
A program may use at most 128 MiB of HBM per device.

```python
import math
import jax
import jax.numpy as jnp
import numpy as np

CX = 256
CY = 64
ITERS = 2
ROWS_DEV = 16384
L = 20
NX = 1024
NY = 128
TILES = 8
CAP = 4096
ROWS = 524288
N_GX = 4
N_GY = 2
N_GZ = 4


def plant(array, rng, low, top_value):
    shape = array.shape
    spot = [jax.random.randint(jax.random.fold_in(rng, axis), (), 0, shape[axis]) for axis in range(len(shape))]
    array = array.at[tuple(spot)].set(low)
    longest = shape.index(max(shape))
    spot[longest] = (spot[longest] + 1) % shape[longest]
    return array.at[tuple(spot)].set(top_value)


def levels(own_key, extent, cuts, low, high):
    factor_of = 1.0
    for dim, blocks in cuts:
        steps = jax.random.uniform(jax.random.fold_in(jax.random.fold_in(own_key, 6), dim), (blocks,), jnp.float32, low / len(cuts), high / len(cuts))
        factor_of = factor_of * jnp.repeat(jnp.exp(steps), extent[dim] // blocks).reshape((-1,) + (1,) * (len(extent) - 1 - dim))
    return factor_of


def split_up(amount, total, limit, skew):
    loads = [(1 << 20) // math.isqrt(grade ** skew) + 1 for grade in range(2, amount + 1)]
    spare, holding = total - limit - (amount - 1), [1] * (amount - 1)
    while spare > 0:
        candidates = [i for i in range(amount - 1) if holding[i] < limit]
        whole, left = sum([loads[i] for i in candidates]), spare
        for i in candidates:
            addition = min(limit - holding[i], max(1, left * loads[i] // whole), spare)
            holding[i] = holding[i] + addition
            spare = spare - addition
    return np.array([limit] + holding)


def ragged_sizes(key, amount, total, most, lean):
    if amount == 2:
        one = jax.random.randint(key, (), max(1, total - most), min(most, total - 1) + 1)
        return jnp.stack([one, total - one])
    sizes = jnp.asarray(split_up(amount, total, most, lean), jnp.int32)
    twos = (amount - 1) // 2
    source_of, sink = sizes[1:1 + 2 * twos:2], sizes[2:2 + 2 * twos:2]
    slack = jnp.minimum(source_of - 1, most - sink)
    passed = jax.random.randint(jax.random.fold_in(key, 1), (twos,), 0, 1 << 20) % (slack + 1)
    sizes = sizes.at[1:1 + 2 * twos:2].set(source_of - passed).at[2:2 + 2 * twos:2].set(sink + passed)
    return sizes[jax.random.permutation(jax.random.fold_in(key, 2), amount)]


def assign_block(own_key, own, number, rows, amount, top, bound, slope):
    sequence = jax.random.permutation(own_key, amount)
    heavy_load, usual = load_shares(amount, rows * top, bound, slope, True), load_shares(amount, rows * top, bound, slope, False)
    places = jnp.arange(amount)

    def named(tallies, turn):
        used = int((tallies > 0).sum())
        fixed = max(1, used // 4)
        moved = fixed + (places - fixed + turn * (used - fixed)) % max(1, amount - fixed)
        return jnp.zeros((amount,), jnp.int32).at[sequence[jnp.where(places < fixed, places, moved)]].set(jnp.asarray(tallies, jnp.int32))

    tallies = jnp.where(number % 4 == 0, named(heavy_load, number // 4), named(usual, number - number // 4 - 1))
    mixed = jax.random.permutation(jax.random.fold_in(own, 3), amount)
    donor, taker = mixed[0:amount // 2 * 2:2], mixed[1:amount // 2 * 2:2]
    slack = jnp.minimum(tallies[donor] - 1, bound - tallies[taker]) // 2
    slack = jnp.where((donor == sequence[0]) | (taker == sequence[0]) | (tallies[taker] == 0), 0, jnp.maximum(slack, 0))
    moved = jax.random.randint(jax.random.fold_in(own, 4), (amount // 2,), 0, 1 << 20) % (slack + 1)
    tallies = tallies.at[donor].add(-moved).at[taker].add(moved)
    labels = jnp.searchsorted(jnp.cumsum(tallies), jnp.arange(rows * top), side="right").astype(jnp.int32)
    table = labels.reshape(top, rows).T
    table = table[jax.random.permutation(jax.random.fold_in(own, 1), rows)]
    turn = jax.random.randint(jax.random.fold_in(own, 2), (rows, 1), 0, top)
    return jnp.take_along_axis(table, (jnp.arange(top)[None, :] + turn) % top, axis=1)


def load_shares(number_of, total, reach, lean, full):
    portions = [(1 << 20) // math.isqrt(standing ** lean) + 1 for standing in range(1, number_of + 1)]
    largest = reach if full else min(reach, max(-(-total // number_of), total * portions[0] // sum(portions)))
    least = 1 if total - largest >= number_of - 1 else 0
    given, rest = [largest] + [least] * (number_of - 1), total - largest - least * (number_of - 1)
    while rest > 0:
        candidates = [i for i in range(1, number_of) if given[i] < largest] or [i for i in range(1, number_of) if given[i] < reach]
        mass, remaining = sum([portions[i] for i in candidates]), rest
        for i in candidates:
            extra = min(reach - given[i], max(1, remaining * portions[i] // mass), rest)
            given[i] = given[i] + extra
            rest = rest - extra
    return np.array(given)


def scatter_about(rng, dims, spread, most, cuts=(), kind=jnp.bfloat16):
    entries = spread * jax.random.normal(rng, dims, jnp.float32)
    if cuts:
        entries = entries * levels(rng, dims, cuts, -0.22, 0.18)
    return jnp.clip(entries, -most, most).astype(kind)


def setup_inputs(seed: int = 0) -> dict:
    seeds = jax.random.split(jax.random.key(seed), 12)
    adjoint_guess = scatter_about(seeds[0], (2, L, NY, NX), 1.0, 6.0, ((1, 4), (2, 2), (3, 4)), jnp.float32)
    viscosity = jnp.clip(jnp.exp(math.log(2.0) - 2.3025851 * jax.random.uniform(seeds[1], (L, NY, NX), jnp.float32) ** levels(seeds[1], (L, NY, NX), ((0, 4), (1, 2), (2, 4)), -0.2, 0.2)), 0.2, 2.0)
    friction = jnp.clip(jnp.exp(math.log(5.0) - 3.218876 * jax.random.uniform(seeds[2], (NY, NX), jnp.float32) ** levels(seeds[2], (NY, NX), ((0, 2), (1, 4)), -0.2, 0.2)), 0.2, 5.0)
    base_velocity = scatter_about(seeds[3], (2, NY, NX), 1.0, 6.0, ((1, 2), (2, 4)), jnp.float32)
    surface_slope = scatter_about(seeds[4], (2, NY, NX), 1.0, 6.0, ((1, 2), (2, 4)), jnp.float32)
    ice_mask = plant((jax.random.randint(seeds[5], (NY, NX), 0, 5) < 4).astype(jnp.int32), jax.random.fold_in(seeds[5], 1), 0, 1)
    pixel_misfit = scatter_about(seeds[6], (ROWS,), 1.0, 6.0, ((0, 32),), jnp.float32)
    pixel_look = jnp.clip(jax.random.uniform(seeds[7], (ROWS,), jnp.float32, -3.140625, 3.140625), -3.140625, 3.140625)
    pixel_tile_keys = jax.random.split(jax.random.fold_in(seeds[8], 1), ROWS // ROWS_DEV)
    pixel_tile_turns = jax.random.permutation(jax.random.fold_in(seeds[8], 3), ROWS // ROWS_DEV)
    pixel_tile = jax.vmap(lambda own, number: assign_block(jax.random.fold_in(seeds[8], 2), own, number, ROWS_DEV, TILES, 1, CAP, 2))(pixel_tile_keys, pixel_tile_turns).reshape((ROWS, 1))
    pixel_cell = plant(jax.random.randint(seeds[9], (ROWS,), 0, CX * CY), jax.random.fold_in(seeds[9], 1), 0, (CX * CY) - 1).astype(jnp.int32)
    pixel_count = ragged_sizes(seeds[10], N_GX * N_GY * N_GZ, N_GX * N_GY * N_GZ * ROWS_DEV * 3 // 4, ROWS_DEV, 2).astype(jnp.int32)
    return dict(adjoint_guess=adjoint_guess, viscosity=viscosity, friction=friction, base_velocity=base_velocity, surface_slope=surface_slope, ice_mask=ice_mask, pixel_misfit=pixel_misfit, pixel_look=pixel_look, pixel_tile=pixel_tile, pixel_cell=pixel_cell, pixel_count=pixel_count)


OMEGA = 0.6
VERTICAL = 4.0


def box_apply(padded, visc_pad, mask_east, mask_north, mask_upper):
    first = padded[0]
    second = padded[1]
    base_a = first[:-1, :-1, :-1]
    base_b = second[:-1, :-1, :-1]
    east_a = (first[:-1, :-1, 1:] - base_a) * mask_east
    east_b = (second[:-1, :-1, 1:] - base_b) * mask_east
    north_a = (first[:-1, 1:, :-1] - base_a) * mask_north
    north_b = (second[:-1, 1:, :-1] - base_b) * mask_north
    upper_a = (first[1:, :-1, :-1] - base_a) * mask_upper
    upper_b = (second[1:, :-1, :-1] - base_b) * mask_upper
    visc_box = visc_pad[:-1, :-1, :-1]
    along_x = visc_box * (4.0 * east_a + 2.0 * north_b) * mask_east
    along_y = visc_box * (4.0 * north_b + 2.0 * east_a) * mask_north
    shear = visc_box * (north_a + east_b)
    shear_x = shear * mask_east
    shear_y = shear * mask_north
    vert_a = VERTICAL * visc_box * upper_a
    vert_b = VERTICAL * visc_box * upper_b
    result_a = (along_x[1:, 1:, :-1] - along_x[1:, 1:, 1:]) + (shear_y[1:, :-1, 1:] - shear_y[1:, 1:, 1:]) + (vert_a[:-1, 1:, 1:] - vert_a[1:, 1:, 1:])
    result_b = (along_y[1:, :-1, 1:] - along_y[1:, 1:, 1:]) + (shear_x[1:, 1:, :-1] - shear_x[1:, 1:, 1:]) + (vert_b[:-1, 1:, 1:] - vert_b[1:, 1:, 1:])
    return jnp.stack([result_a, result_b])


def reference(adjoint_guess, viscosity, friction, base_velocity, surface_slope, ice_mask, pixel_misfit, pixel_look, pixel_tile, pixel_cell, pixel_count):
    mask_float = ice_mask.astype(jnp.float32)
    row_ids = jnp.arange(ROWS, dtype=jnp.int32)
    device_ids = row_ids // ROWS_DEV
    live = (row_ids % ROWS_DEV) < pixel_count[device_ids]
    values = jnp.where(live, pixel_misfit, jnp.float32(0.0))
    force_x = values * jnp.cos(pixel_look)
    force_y = values * jnp.sin(pixel_look)
    tile_ids = pixel_tile[:, 0]
    col_x = (tile_ids // N_GY) * CX + pixel_cell % CX
    col_y = (tile_ids % N_GY) * CY + pixel_cell // CX
    forcing = jnp.zeros((2, NY, NX), jnp.float32)
    forcing = forcing.at[0, col_y, col_x].add(force_x).at[1, col_y, col_x].add(force_y)
    forcing = forcing * mask_float[None]
    layer_ids = jnp.arange(L, dtype=jnp.int32)
    bottom = (layer_ids == 0).astype(jnp.float32)[:, None, None]
    top = (layer_ids == L - 1).astype(jnp.float32)[:, None, None]
    rhs = forcing[:, None, :, :] * top[None]
    basal = friction[None] * bottom
    damping = OMEGA / (18.0 * viscosity + basal)
    east_ids = jnp.arange(NX + 1, dtype=jnp.int32) - 1
    north_ids = jnp.arange(NY + 1, dtype=jnp.int32) - 1
    upper_ids = jnp.arange(L + 1, dtype=jnp.int32) - 1
    mask_east = (east_ids + 1 < NX).astype(jnp.float32)[None, None, :]
    mask_north = (north_ids + 1 < NY).astype(jnp.float32)[None, :, None]
    mask_upper = (upper_ids + 1 < L).astype(jnp.float32)[:, None, None]
    visc_pad = jnp.pad(viscosity, 1)
    adjoint = adjoint_guess
    for sweep in range(ITERS):
        padded = jnp.pad(adjoint, ((0, 0), (1, 1), (1, 1), (1, 1)))
        image = box_apply(padded, visc_pad, mask_east, mask_north, mask_upper) + basal[None] * adjoint
        adjoint = adjoint + damping[None] * (rhs - image)
    fric_map = -mask_float * friction * (base_velocity[0] * adjoint[0, 0] + base_velocity[1] * adjoint[1, 0])
    drive_map = 0.25 * mask_float * jnp.sum(surface_slope[0][None] * adjoint[0] + surface_slope[1][None] * adjoint[1], axis=0)
    return adjoint, jnp.stack([fric_map, drive_map])
```

```python
import functools
import math

import jax
import jax.numpy as jnp
from jax import lax
from jax.experimental import pallas as pl
from jax.experimental.pallas import tpu as pltpu
from jax.sharding import PartitionSpec as P

GROUPS = 4
SLOT_TILES = 8
DEPTH = 1024


def lane_column(pack, lane, like):
    return jnp.broadcast_to(pack[:, lane : lane + 1], like.shape)


def from_east(value, column):
    size = value.shape[1]
    lanes = lax.broadcasted_iota(jnp.int32, value.shape, 1)
    return jnp.where(lanes == size - 1, column, pltpu.roll(value, size - 1, 1))


def from_west(value, column):
    lanes = lax.broadcasted_iota(jnp.int32, value.shape, 1)
    return jnp.where(lanes == 0, column, pltpu.roll(value, 1, 1))


def from_north(value, row):
    size = value.shape[0]
    rows = lax.broadcasted_iota(jnp.int32, value.shape, 0)
    return jnp.where(rows == size - 1, row, pltpu.roll(value, size - 1, 0))


def from_south(value, row):
    rows = lax.broadcasted_iota(jnp.int32, value.shape, 0)
    return jnp.where(rows == 0, row, pltpu.roll(value, 1, 0))


def reverse_bits(value, bits):
    out = 0
    for bit in range(bits):
        out |= ((value >> bit) & 1) << (bits - 1 - bit)
    return out


def sin_cos(angle):
    turns = jnp.floor(angle * (2.0 / math.pi) + 0.5)
    rest = angle - turns * 1.5703125
    rest = rest - turns * 4.837512969970703125e-4
    rest = rest - turns * 7.54978995489188e-8
    square = rest * rest
    sine = -1.9515295891e-4 * square + 8.3321608736e-3
    sine = (sine * square - 1.6666654611e-1) * square * rest + rest
    cosine = 2.443315711809948e-5 * square - 1.388731625493765e-3
    cosine = (cosine * square + 4.166664568298827e-2) * square * square
    cosine = cosine - 0.5 * square + 1.0
    quadrant = turns.astype(jnp.int32) & 3
    swap = (quadrant & 1) == 1
    first = jnp.where(swap, cosine, sine)
    second = jnp.where(swap, sine, cosine)
    out_sine = jnp.where(quadrant >= 2, -first, first)
    out_cosine = jnp.where((quadrant == 1) | (quadrant == 2), -second, second)
    return out_sine, out_cosine


def apply_kernel(
    counts,
    count_ref,
    misfit_ref,
    look_ref,
    tile_ref,
    cell_ref,
    guess,
    visc,
    fric,
    base,
    slope,
    mask,
    adj_out,
    maps_out,
    *scratch,
):
    nx, ny, nz = counts
    bits = nz.bit_length() - 1
    tiles = nx * ny
    layers, rows, cols = visc.shape
    size = rows // nz
    groups = GROUPS if tiles % GROUPS == 0 else 1
    per = tiles // groups
    scratch = list(scratch)
    accs = [scratch.pop(0) for _ in range(bits)]
    recvs = [scratch.pop(0) for _ in range(bits)]
    (
        pixels,
        sums,
        lhs,
        rhs,
        acc,
        tile_in,
        block,
        forcing,
        middle,
        west_edge,
        east_edge,
        south_edge,
        north_edge,
        halo_w,
        halo_e,
        halo_s,
        halo_n,
        halo_se,
        halo_nw,
        halo_d,
        halo_u,
        visc_d,
        part,
        part_in,
        edge_w,
        edge_e,
        edge_s,
        edge_n,
        ring_w,
        ring_e,
        ring_s,
        ring_n,
        ring_se,
        ring_nw,
        late,
        late_in,
        half_sem,
        tile_sem,
        last_send,
        last_recv,
        halo_sem,
        visc_sem,
        part_sem,
        ring_send,
        ring_recv,
        late_sem,
    ) = scratch
    steps, _, depth = pixels.shape[1:]
    gx, gy, gz = lax.axis_index("gx"), lax.axis_index("gy"), lax.axis_index("gz")
    tile = gx * ny + gy
    lane_step = 16
    row_step = 8
    top = nz - 1

    def remote(src, dst, send, recv, device):
        return pltpu.make_async_remote_copy(
            src_ref=src,
            dst_ref=dst,
            send_sem=send,
            recv_sem=recv,
            device_id=device,
            device_id_type=pl.DeviceIdType.MESH,
        )

    barrier = pltpu.get_barrier_semaphore()
    layer_peers = [(gx, gy, lax.rem(gz + o, nz)) for o in range(1, nz)]
    tile_peers = []
    for o in range(1, tiles):
        other = lax.rem(tile + o, tiles)
        tile_peers.append((other, (lax.div(other, ny), lax.rem(other, ny), gz)))
    for device in layer_peers + [device for _, device in tile_peers]:
        pl.semaphore_signal(barrier, inc=1, device_id=device, device_id_type=pl.DeviceIdType.MESH)

    def prepare():
        sine, cosine = sin_cos(look_ref[...])
        order = lax.broadcasted_iota(jnp.int32, misfit_ref.shape, 0) * misfit_ref.shape[1]
        order = order + lax.broadcasted_iota(jnp.int32, misfit_ref.shape, 1)
        value = jnp.where(order < count_ref[0], misfit_ref[...], 0.0)
        cell = cell_ref[...]
        row = lax.div(cell, cols)
        fields = []
        for f in (value * cosine, value * sine):
            high = f.astype(jnp.bfloat16).astype(jnp.float32)
            fields += [high, f - high]
        fields.append((tile_ref[...] * rows + row).astype(jnp.float32))
        fields.append((cell - row * cols).astype(jnp.float32))
        lanes = misfit_ref.shape[1]
        width = depth // lanes
        for f, field in enumerate(fields):
            for r in range(steps * width):
                begin = (r % width) * lanes
                pixels[f, r // width, :, begin : begin + lanes] = field[r : r + 1, :]

    starts = []
    length = nz // 2
    for bit in range(bits):
        own_bit = lax.rem(lax.div(gz, 1 << bit), 2)
        keep = own_bit * length
        give = (1 - own_bit) * length
        peer = (gx, gy, gz + (1 - 2 * own_bit) * (1 << bit))
        starts.append((keep, give, length, peer))
        length //= 2

    def half_copy(bit, g):
        _, give, length, peer = starts[bit]
        source = sums if bit == 0 else accs[bit - 1]
        own = pl.ds(g * per, per)
        return remote(
            source.at[pl.ds(give, length), own],
            recvs[bit].at[:, own],
            half_sem.at[0, bit, g],
            half_sem.at[1, bit, g],
            peer,
        )

    def bin_group(g):
        acc[...] = jnp.zeros_like(acc)

        def step(i, slot):
            if g == 0:
                ids = lax.broadcasted_iota(jnp.int32, (cols, depth), 0)
                ids = ids.astype(jnp.float32).astype(jnp.bfloat16)
                col = pixels[5, i].astype(jnp.bfloat16)
                one = jnp.ones((cols, depth), jnp.bfloat16)
                rhs[i] = jnp.where(ids == col, one, jnp.zeros_like(one))
            pieces = [pixels[f, i].astype(jnp.bfloat16) for f in range(4)]
            row = pixels[4, i]
            ids = lax.broadcasted_iota(jnp.int32, (rows, depth), 0)
            ids = ids.astype(jnp.float32).astype(jnp.bfloat16)
            zero = jnp.zeros((rows, depth), jnp.bfloat16)
            for n in range(per):
                own = (row - float((g * per + n) * rows)).astype(jnp.bfloat16)
                hit = ids == own
                for c in range(2):
                    for part_id in range(2):
                        start = ((part_id * per + n) * 2 + c) * rows
                        piece = jnp.broadcast_to(pieces[2 * c + part_id], (rows, depth))
                        lhs[slot, start : start + rows, :] = jnp.where(hit, piece, zero)
            acc[...] += lax.dot_general(
                lhs[slot], rhs[i], (((1,), (1,)), ((), ())), preferred_element_type=jnp.float32
            )

        def several(j, carry):
            for slot in range(unroll):
                step(j * unroll + slot, slot)
            return carry

        unroll = lhs.shape[0]
        lax.fori_loop(0, steps // unroll, several, 0)
        half = per * 2 * rows
        for n in range(per):
            for c in range(2):
                for q in range(nz):
                    begin = (n * 2 + c) * rows + q * size
                    sums[reverse_bits(q, bits), g * per + n, c] = (
                        acc[begin : begin + size] + acc[half + begin : half + begin + size]
                    )

    def pack(field):
        lanes = lax.broadcasted_iota(jnp.int32, (rows, 128), 1)
        west = jnp.zeros((rows, 128), jnp.float32)
        east = jnp.zeros((rows, 128), jnp.float32)
        for f in range(3):
            for k in range(layers):
                value = field[f, k] if f < 2 else visc[k]
                south_edge[f * row_step + k : f * row_step + k + 1, :] = value[0:1, :]
                north_edge[f * row_step + k : f * row_step + k + 1, :] = value[rows - 1 : rows, :]
                lane = lanes == f * lane_step + k
                west = jnp.where(lane, lane_column(value, 0, west), west)
                east = jnp.where(lane, lane_column(value, cols - 1, east), east)
        west_edge[...] = west
        east_edge[...] = east

    def halo_copies(field, turn):
        def one(index, src, dst, device):
            return remote(src, dst, halo_sem.at[turn, 0, index], halo_sem.at[turn, 1, index], device)

        return [
            (one(0, west_edge, halo_e.at[turn], (gx - 1, gy, gz)), gx > 0, gx < nx - 1),
            (one(1, east_edge, halo_w.at[turn], (gx + 1, gy, gz)), gx < nx - 1, gx > 0),
            (one(2, south_edge, halo_n.at[turn], (gx, gy - 1, gz)), gy > 0, gy < ny - 1),
            (one(3, north_edge, halo_s.at[turn], (gx, gy + 1, gz)), gy < ny - 1, gy > 0),
            (
                one(4, north_edge.at[:, 0:128], halo_se.at[turn], (gx - 1, gy + 1, gz)),
                (gx > 0) & (gy < ny - 1),
                (gx < nx - 1) & (gy > 0),
            ),
            (
                one(5, east_edge.at[0:8, :], halo_nw.at[turn], (gx + 1, gy - 1, gz)),
                (gx < nx - 1) & (gy > 0),
                (gx > 0) & (gy < ny - 1),
            ),
            (one(6, field.at[:, 0], halo_u.at[turn], (gx, gy, gz - 1)), gz > 0, gz < nz - 1),
            (one(7, field.at[:, layers - 1], halo_d.at[turn], (gx, gy, gz + 1)), gz < nz - 1, gz > 0),
        ]

    def start_all(copies):
        for copy, sends, _ in copies:

            @pl.when(sends)
            def _(copy=copy):
                copy.start()

    def wait_receives(copies):
        for copy, _, receives in copies:

            @pl.when(receives)
            def _(copy=copy):
                copy.wait_recv()

    def wait_sends(copies):
        for copy, sends, _ in copies:

            @pl.when(sends)
            def _(copy=copy):
                copy.wait_send()

    lane_ids = lax.broadcasted_iota(jnp.int32, (rows, cols), 1)
    row_ids = lax.broadcasted_iota(jnp.int32, (rows, cols), 0)

    def masks():
        mx = jnp.where((lane_ids < cols - 1) | (gx < nx - 1), 1.0, 0.0)
        my = jnp.where((row_ids < rows - 1) | (gy < ny - 1), 1.0, 0.0)
        return mx, my

    west_on = jnp.where(gx > 0, 1.0, 0.0)
    south_on = jnp.where(gy > 0, 1.0, 0.0)
    up_on = jnp.where(gz < nz - 1, 1.0, 0.0)

    def damping_of(k):
        scale = 18.0 * visc[k]
        if k == 0:
            scale = scale + jnp.where(gz == 0, fric[...], 0.0)
        return 0.6 / scale

    def west_stress(a, b, v, corner_a, corner_b, own_a, own_b, my_col):
        na = (from_north(a, corner_a) - a) * my_col
        nb = (from_north(b, corner_b) - b) * my_col
        ea = (own_a - a) * west_on
        eb = (own_b - b) * west_on
        return v * (4.0 * ea + 2.0 * nb) * west_on, v * (na + eb) * west_on

    def south_stress(a, b, v, corner_a, corner_b, own_a, own_b, mx_row):
        ea = (from_east(a, corner_a) - a) * mx_row
        eb = (from_east(b, corner_b) - b) * mx_row
        na = (own_a - a) * south_on
        nb = (own_b - b) * south_on
        return v * (4.0 * nb + 2.0 * ea) * south_on, v * (na + eb) * south_on

    def plane_image(va, vb, v, east_a, east_b, north_a, north_b, col_p, col_s, row_q, row_s, mx, my):
        ea = (from_east(va, east_a) - va) * mx
        eb = (from_east(vb, east_b) - vb) * mx
        na = (from_north(va, north_a) - va) * my
        nb = (from_north(vb, north_b) - vb) * my
        p = mx * v * (4.0 * ea + 2.0 * nb)
        q = my * v * (4.0 * nb + 2.0 * ea)
        s = v * (na + eb)
        sx = mx * s
        sy = my * s
        image_a = (from_west(p, col_p) - p) + (from_south(sy, row_s) - sy)
        image_b = (from_south(q, row_q) - q) + (from_west(sx, col_s) - sx)
        return image_a, image_b

    def sweep(field, turn, store):
        mx, my = masks()
        my_col = my[:, 0:128]
        mx_row = mx[0:8, :]
        west = jnp.where(gx > 0, halo_w[turn], 0.0)
        east = jnp.where(gx < nx - 1, halo_e[turn], 0.0)
        south = jnp.where(gy > 0, halo_s[turn], 0.0)
        north = jnp.where(gy < ny - 1, halo_n[turn], 0.0)
        corner_se = jnp.where((gx < nx - 1) & (gy > 0), halo_se[turn], 0.0)
        corner_nw = jnp.where((gx > 0) & (gy < ny - 1), halo_nw[turn], 0.0)
        own_w = west_edge[...]
        own_s = south_edge[...]
        corner_b = pltpu.roll(corner_nw, 128 - lane_step, 1)
        col_p, col_s = west_stress(
            west,
            pltpu.roll(west, 128 - lane_step, 1),
            pltpu.roll(west, 128 - 2 * lane_step, 1),
            corner_nw[0:1, :],
            corner_b[0:1, :],
            own_w,
            pltpu.roll(own_w, 128 - lane_step, 1),
            my_col,
        )
        south_a, south_b, south_v = south[0:8], south[8:16], south[16:24]
        row_q, row_s = south_stress(
            south_a,
            south_b,
            south_v,
            lane_column(corner_se[0:8], 0, south_a),
            lane_column(corner_se[8:16], 0, south_b),
            own_s[0:8],
            own_s[8:16],
            mx_row,
        )

        below_v = jnp.where(gz > 0, visc_d[...], 0.0)
        low_a = 4.0 * below_v * (field[0, 0] - jnp.where(gz > 0, halo_d[turn, 0], 0.0))
        low_b = 4.0 * below_v * (field[1, 0] - jnp.where(gz > 0, halo_d[turn, 1], 0.0))
        for k in range(layers):
            va, vb, v = field[0, k], field[1, k], visc[k]
            if k < layers - 1:
                top_a = 4.0 * v * (field[0, k + 1] - va)
                top_b = 4.0 * v * (field[1, k + 1] - vb)
            else:
                top_a = 4.0 * v * (jnp.where(gz < nz - 1, halo_u[turn, 0], 0.0) - va) * up_on
                top_b = 4.0 * v * (jnp.where(gz < nz - 1, halo_u[turn, 1], 0.0) - vb) * up_on
            image_a, image_b = plane_image(
                va,
                vb,
                v,
                lane_column(east, k, va),
                lane_column(east, lane_step + k, vb),
                north[k : k + 1],
                north[row_step + k : row_step + k + 1],
                lane_column(col_p, k, va),
                lane_column(col_s, k, va),
                row_q[k : k + 1],
                row_s[k : k + 1],
                mx,
                my,
            )
            image_a = image_a + (low_a - top_a)
            image_b = image_b + (low_b - top_b)
            if k == 0:
                basal = jnp.where(gz == 0, fric[...], 0.0)
                image_a = image_a + basal * va
                image_b = image_b + basal * vb
            low_a, low_b = top_a, top_b
            damp = damping_of(k)
            store(k, va - damp * image_a, vb - damp * image_b)

    def store_first(k, new_a, new_b):
        middle[0, k] = new_a
        middle[1, k] = new_b

    def store_second(k, new_a, new_b):
        adj_out[0, k] = new_a
        adj_out[1, k] = new_b
        term = slope[0] * new_a + slope[1] * new_b
        if k == 0:
            on_base = jnp.where(gz == 0, 1.0, 0.0)
            land = mask[...].astype(jnp.float32)
            part[0] = -on_base * land * fric[...] * (base[0] * new_a + base[1] * new_b)
            part[1] = term
        elif k < layers - 1:
            part[1] = part[1] + term
        else:
            part[1] = 0.25 * mask[...].astype(jnp.float32) * (part[1] + term)

    def tile_copy(t):
        device = (t // ny, t % ny, gz)
        return remote(
            total.at[0, t], tile_in.at[tile], tile_sem.at[0, t], tile_sem.at[1, tile], device
        )

    def finish(bit, g):
        keep, give, length, _ = starts[bit]
        source = sums if bit == 0 else accs[bit - 1]
        own = pl.ds(g * per, per)
        half_copy(bit, g).wait_recv()
        if bit + 1 < bits:
            next_keep, next_give, next_length, _ = starts[bit + 1]
            for begin in (next_give, next_keep):
                accs[bit][pl.ds(begin, next_length), own] = (
                    source[pl.ds(keep + begin, next_length), own]
                    + recvs[bit][pl.ds(begin, next_length), own]
                )
                if begin is next_give:
                    half_copy(bit + 1, g).start()
            return
        accs[bit][:, own] = source[pl.ds(keep, length), own] + recvs[bit][:, own]
        for t in range(g * per, (g + 1) * per):

            @pl.when(tile != t)
            def _(t=t):
                tile_copy(t).start()

            @pl.when(tile == t)
            def _(t=t):
                tile_in[t] = total[0, t]

    total = accs[bits - 1]

    def part_copy(o):
        device = layer_peers[o - 1]
        begin = pl.multiple_of(device[2] * size, size)
        return remote(
            part.at[:, pl.ds(begin, size), :],
            part_in.at[o - 1],
            part_sem.at[0, o - 1],
            part_sem.at[1, o - 1],
            device,
        )

    prepare()
    bin_group(0)
    pl.semaphore_wait(barrier, nz - 1 + tiles - 1)
    half_copy(0, 0).start()
    visc_up = (
        remote(visc.at[layers - 1], visc_d, visc_sem.at[0], visc_sem.at[1], (gx, gy, gz + 1)),
        gz < nz - 1,
        gz > 0,
    )
    pack(guess)
    first = halo_copies(guess, 0) + [visc_up]
    second = halo_copies(middle, 1)
    start_all(first)

    def early(turn):
        if turn == 3:
            wait_receives(first)
            wait_sends(first)
            sweep(guess, 0, store_first)
            pack(middle)
            start_all(second)
        elif turn == 5:
            wait_receives(second)
            sweep(middle, 1, store_second)
            for o in range(1, nz):
                part_copy(o).start()
            wait_sends(second)

    for turn in range(1, groups + bits):
        if turn < groups:
            bin_group(turn)
            half_copy(0, turn).start()
        for bit in reversed(range(bits)):
            g = turn - 1 - bit
            if 0 <= g < groups:
                finish(bit, g)
        early(turn)
    for turn in range(groups + bits, 3):
        early(turn)
    for t in range(tiles):

        @pl.when(tile != t)
        def _(t=t):
            remote(
                total.at[0, t], tile_in.at[t], tile_sem.at[0, t], tile_sem.at[1, t], (t // ny, t % ny, gz)
            ).wait_recv()

    own_rows = pl.ds(pl.multiple_of(gz * size, size), size)
    value = tile_in[0]
    for t in range(1, tiles):
        value = value + tile_in[t]
    land = mask[own_rows, :].astype(jnp.float32)
    value = value * land[None]
    block[...] = value

    lanes = lax.broadcasted_iota(jnp.int32, (size, 128), 1)
    west = jnp.zeros((size, 128), jnp.float32)
    east = jnp.zeros((size, 128), jnp.float32)
    for c in range(2):
        west = jnp.where(lanes == c * lane_step, lane_column(value[c], 0, west), west)
        east = jnp.where(lanes == c * lane_step, lane_column(value[c], cols - 1, east), east)
        edge_s[c * row_step : c * row_step + 1, :] = value[c, 0:1, :]
        edge_n[c * row_step : c * row_step + 1, :] = value[c, size - 1 : size, :]
    edge_w[...] = west
    edge_e[...] = east

    is_top = gz == top
    low = gz == 0

    def ring_one(index, src, dst, slot, device):
        return remote(src, dst, ring_send.at[index], ring_recv.at[slot], device)

    def ring_column(index, src, ring, q, device, slot):
        return ring_one(index, src, ring.at[q], slot, device)

    ring_sends = [
        (ring_one(0, edge_w, ring_e.at[gz], gz, (gx - 1, gy, top)), gx > 0),
        (ring_one(1, edge_e, ring_w.at[gz], nz + gz, (gx + 1, gy, top)), gx < nx - 1),
        (ring_one(2, edge_s, ring_n, 2 * nz, (gx, gy - 1, top)), low & (gy > 0)),
        (ring_one(3, edge_n, ring_s, 2 * nz + 1, (gx, gy + 1, top)), is_top & (gy < ny - 1)),
        (
            ring_one(4, edge_n.at[:, 0:128], ring_se, 2 * nz + 2, (gx - 1, gy + 1, top)),
            is_top & (gx > 0) & (gy < ny - 1),
        ),
        (
            ring_one(5, edge_e.at[0:8, :], ring_nw, 2 * nz + 3, (gx + 1, gy - 1, top)),
            low & (gx < nx - 1) & (gy > 0),
        ),
    ]
    for copy, sends in ring_sends:

        @pl.when(sends)
        def _(copy=copy):
            copy.start()

    to_last = remote(block, forcing.at[gz], last_send, last_recv.at[gz], (gx, gy, top))

    @pl.when(gz < top)
    def _():
        to_last.start()

    def late_copy(j):
        return remote(late.at[j], late_in, late_sem.at[0, j], late_sem.at[1, 0], (gx, gy, j))

    gathered = part[:, own_rows, :]
    for o in range(1, nz):
        part_copy(o).wait_recv()
        gathered = gathered + part_in[o - 1]
    maps_out[...] = gathered

    @pl.when(is_top)
    def _():
        forcing[top] = block[...]
        for j in range(top):
            remote(block, forcing.at[j], last_send, last_recv.at[j], (gx, gy, 0)).wait_recv()
        peer = (lax.rem(gx + 1, nx), gy, top)
        for j in range(nz):

            @pl.when(gx < nx - 1)
            def _(j=j):
                ring_one(0, edge_w, ring_e.at[j], j, peer).wait_recv()

            @pl.when(gx > 0)
            def _(j=j):
                ring_one(1, edge_e, ring_w.at[j], nz + j, peer).wait_recv()

        @pl.when(gy < ny - 1)
        def _():
            ring_one(2, edge_s, ring_n, 2 * nz, peer).wait_recv()

        @pl.when(gy > 0)
        def _():
            ring_one(3, edge_n, ring_s, 2 * nz + 1, peer).wait_recv()

        @pl.when((gx < nx - 1) & (gy > 0))
        def _():
            ring_one(4, edge_n.at[:, 0:128], ring_se, 2 * nz + 2, peer).wait_recv()

        @pl.when((gx > 0) & (gy < ny - 1))
        def _():
            ring_one(5, edge_e.at[0:8, :], ring_nw, 2 * nz + 3, peer).wait_recv()

        mx, my = masks()
        my_col = my[:, 0:128]
        mx_row = mx[0:8, :]
        last = layers - 1
        shift = 128 - 2 * lane_step - last

        def scaled(on, force, v):
            return jnp.where(on, force * (0.6 / (18.0 * v)), 0.0)

        def columns(value):
            a = lane_column(value, 0, value)
            return a, lane_column(value, lane_step, value)

        v = visc[last]
        damp = damping_of(last)
        force_a = jnp.concatenate([forcing[q, 0] for q in range(nz)], axis=0)
        force_b = jnp.concatenate([forcing[q, 1] for q in range(nz)], axis=0)
        ea = damp * force_a
        eb = damp * force_b

        west_v = lane_column(halo_w[0], 2 * lane_step + last, halo_w[0])
        east_v = lane_column(halo_e[0], 2 * lane_step + last, halo_e[0])
        south_v = jnp.broadcast_to(halo_s[0, 16 + last : 17 + last, :], (8, cols))
        north_v = jnp.broadcast_to(halo_n[0, 16 + last : 17 + last, :], (8, cols))
        nw_v = lane_column(halo_nw[0], 2 * lane_step + last, halo_nw[0])
        se_v = jnp.broadcast_to(halo_se[0, 16 + last : 17 + last, :], (8, 128))

        ring_w_all = jnp.concatenate([ring_w[q] for q in range(nz)], axis=0)
        ring_e_all = jnp.concatenate([ring_e[q] for q in range(nz)], axis=0)
        west_a, west_b = [scaled(gx > 0, f, west_v) for f in columns(ring_w_all)]
        east_a, east_b = [scaled(gx < nx - 1, f, east_v) for f in columns(ring_e_all)]
        nw_on = (gx > 0) & (gy < ny - 1)
        se_on = (gx < nx - 1) & (gy > 0)
        nw_a, nw_b = [scaled(nw_on, f, nw_v) for f in columns(ring_nw[...])]
        south_a = scaled(gy > 0, ring_s[0:8], south_v)
        south_b = scaled(gy > 0, ring_s[8:16], south_v)
        north_a = scaled(gy < ny - 1, ring_n[0:8], north_v)
        north_b = scaled(gy < ny - 1, ring_n[8:16], north_v)
        se_a = scaled(se_on, ring_se[0:8], se_v)
        se_b = scaled(se_on, ring_se[8:16], se_v)
        west_v = jnp.where(gx > 0, west_v, 0.0)
        south_v = jnp.where(gy > 0, south_v, 0.0)

        col_p, col_s = west_stress(
            west_a,
            west_b,
            west_v,
            nw_a[0:1, :],
            nw_b[0:1, :],
            lane_column(ea, 0, west_a),
            lane_column(eb, 0, west_b),
            my_col,
        )
        row_q, row_s = south_stress(
            south_a,
            south_b,
            south_v,
            lane_column(se_a, 0, south_a),
            lane_column(se_b, 0, south_b),
            jnp.broadcast_to(ea[0:1, :], south_a.shape),
            jnp.broadcast_to(eb[0:1, :], south_b.shape),
            mx_row,
        )
        image_a, image_b = plane_image(
            ea,
            eb,
            v,
            lane_column(east_a, 0, ea),
            lane_column(east_b, 0, eb),
            north_a[0:1],
            north_b[0:1],
            lane_column(col_p, 0, ea),
            lane_column(col_s, 0, ea),
            row_q[0:1],
            row_s[0:1],
            mx,
            my,
        )
        below = 4.0 * visc[last - 1]
        image_a = image_a + below * ea
        image_b = image_b + below * eb
        top_a = ea + damp * (force_a - image_a)
        top_b = eb + damp * (force_b - image_b)
        lift = damping_of(last - 1) * below
        low_a = lift * ea
        low_b = lift * eb
        land = mask[...].astype(jnp.float32)
        drive = 0.25 * land * (slope[0] * (top_a + low_a) + slope[1] * (top_b + low_b))
        for j in range(nz):
            late[j] = drive[j * size : (j + 1) * size, :]
        for j in range(top):
            late_copy(j).start()
        adj_out[0, last] = adj_out[0, last] + top_a
        adj_out[1, last] = adj_out[1, last] + top_b
        adj_out[0, last - 1] = adj_out[0, last - 1] + low_a
        adj_out[1, last - 1] = adj_out[1, last - 1] + low_b
        maps_out[1] = maps_out[1] + late[top]
        for j in range(top):
            late_copy(j).wait_send()

    @pl.when(gz < top)
    def _():
        remote(late.at[0], late_in, late_sem.at[0, 0], late_sem.at[1, 0], (gx, gy, top)).wait_recv()
        maps_out[1] = maps_out[1] + late_in[...]

    for bit in range(bits):
        for g in range(groups):
            half_copy(bit, g).wait_send()
    for t in range(tiles):

        @pl.when(tile != t)
        def _(t=t):
            tile_copy(t).wait_send()

    @pl.when(gz < top)
    def _():
        to_last.wait_send()

    for copy, sends in ring_sends:

        @pl.when(sends)
        def _(copy=copy):
            copy.wait_send()

    for o in range(1, nz):
        part_copy(o).wait_send()


def apply_twice(count, pixels, guess, visc, fric, base, slope, mask, counts):
    nx, ny, nz = counts
    tiles = nx * ny
    bits = nz.bit_length() - 1
    _, layers, rows, cols = guess.shape
    size = rows // nz
    f32 = jnp.float32
    groups = GROUPS if tiles % GROUPS == 0 else 1
    per = tiles // groups
    per_device = pixels[0].shape[0]
    depth = min(DEPTH, per_device)
    steps = per_device // depth
    flat = [value.reshape(per_device // 128, 128) for value in pixels]
    slots = math.gcd(steps, max(1, SLOT_TILES // per))
    halves = [pltpu.VMEM((nz >> (bit + 1), tiles, 2, size, cols), f32) for bit in range(bits)]
    vmem = pl.BlockSpec(memory_space=pltpu.VMEM)
    dma = pltpu.SemaphoreType.DMA
    return pl.pallas_call(
        functools.partial(apply_kernel, counts),
        in_specs=[pl.BlockSpec(memory_space=pltpu.SMEM)] + [vmem] * 10,
        out_specs=(vmem, vmem),
        out_shape=(pltpu.VMEM(guess.shape, f32), pltpu.VMEM((2, size, cols), f32)),
        scratch_shapes=halves
        + halves
        + [
            pltpu.VMEM((6, steps, 1, depth), f32),
            pltpu.VMEM((nz, tiles, 2, size, cols), f32),
            pltpu.VMEM((slots, per * 4 * rows, depth), jnp.bfloat16),
            pltpu.VMEM((steps, cols, depth), jnp.bfloat16),
            pltpu.VMEM((per * 4 * rows, cols), f32),
            pltpu.VMEM((tiles, 2, size, cols), f32),
            pltpu.VMEM((2, size, cols), f32),
            pltpu.VMEM((nz, 2, size, cols), f32),
            pltpu.VMEM(guess.shape, f32),
            pltpu.VMEM((rows, 128), f32),
            pltpu.VMEM((rows, 128), f32),
            pltpu.VMEM((24, cols), f32),
            pltpu.VMEM((24, cols), f32),
            pltpu.VMEM((2, rows, 128), f32),
            pltpu.VMEM((2, rows, 128), f32),
            pltpu.VMEM((2, 24, cols), f32),
            pltpu.VMEM((2, 24, cols), f32),
            pltpu.VMEM((2, 24, 128), f32),
            pltpu.VMEM((2, 8, 128), f32),
            pltpu.VMEM((2, 2, rows, cols), f32),
            pltpu.VMEM((2, 2, rows, cols), f32),
            pltpu.VMEM((rows, cols), f32),
            pltpu.VMEM((2, rows, cols), f32),
            pltpu.VMEM((nz - 1, 2, size, cols), f32),
            pltpu.VMEM((size, 128), f32),
            pltpu.VMEM((size, 128), f32),
            pltpu.VMEM((16, cols), f32),
            pltpu.VMEM((16, cols), f32),
            pltpu.VMEM((nz, size, 128), f32),
            pltpu.VMEM((nz, size, 128), f32),
            pltpu.VMEM((16, cols), f32),
            pltpu.VMEM((16, cols), f32),
            pltpu.VMEM((16, 128), f32),
            pltpu.VMEM((8, 128), f32),
            pltpu.VMEM((nz, size, cols), f32),
            pltpu.VMEM((size, cols), f32),
            dma((2, bits, groups)),
            dma((2, tiles)),
            dma,
            dma((nz,)),
            dma((2, 2, 8)),
            dma((2,)),
            dma((2, nz - 1)),
            dma((6,)),
            dma((2 * nz + 4,)),
            dma((2, nz)),
        ],
        compiler_params=pltpu.CompilerParams(
            collective_id=0, has_side_effects=True, vmem_limit_bytes=56 * 2**20
        ),
        name="apply_twice",
    )(count, *flat, guess, visc, fric, base, slope, mask)


def body(
    adjoint_guess,
    viscosity,
    friction,
    base_velocity,
    surface_slope,
    ice_mask,
    pixel_misfit,
    pixel_look,
    pixel_tile,
    pixel_cell,
    pixel_count,
):
    sizes = tuple(lax.axis_size(name) for name in ("gx", "gy", "gz"))
    pixels = (pixel_misfit, pixel_look, pixel_tile[:, 0], pixel_cell)
    return apply_twice(
        pixel_count,
        pixels,
        adjoint_guess,
        viscosity,
        friction,
        base_velocity,
        surface_slope,
        ice_mask,
        sizes,
    )


def solution(mesh):
    return jax.shard_map(
        body,
        mesh=mesh,
        in_specs=(
            P(None, "gz", "gy", "gx"),
            P("gz", "gy", "gx"),
            P("gy", "gx"),
            P(None, "gy", "gx"),
            P(None, "gy", "gx"),
            P("gy", "gx"),
            P(("gx", "gy", "gz")),
            P(("gx", "gy", "gz")),
            P(("gx", "gy", "gz"), None),
            P(("gx", "gy", "gz")),
            P(("gx", "gy", "gz")),
        ),
        out_specs=(P(None, "gz", "gy", "gx"), P(None, ("gy", "gz"), "gx")),
        check_vma=False,
    )
```

```python
import functools
import math

import jax
import jax.numpy as jnp
from jax import lax
from jax.experimental import pallas as pl
from jax.experimental.pallas import tpu as pltpu
from jax.sharding import PartitionSpec as P

SHARES = (3, 2, 2, 1)
FIRST = -1


def lane_column(pack, lane, like):
    return jnp.broadcast_to(pack[:, lane : lane + 1], like.shape)


def from_east(value, column):
    size = value.shape[1]
    lanes = lax.broadcasted_iota(jnp.int32, value.shape, 1)
    return jnp.where(lanes == size - 1, column, pltpu.roll(value, size - 1, 1))


def from_west(value, column):
    lanes = lax.broadcasted_iota(jnp.int32, value.shape, 1)
    return jnp.where(lanes == 0, column, pltpu.roll(value, 1, 1))


def from_north(value, row):
    size = value.shape[0]
    rows = lax.broadcasted_iota(jnp.int32, value.shape, 0)
    return jnp.where(rows == size - 1, row, pltpu.roll(value, size - 1, 0))


def from_south(value, row):
    rows = lax.broadcasted_iota(jnp.int32, value.shape, 0)
    return jnp.where(rows == 0, row, pltpu.roll(value, 1, 0))


def reverse_bits(value, bits):
    out = 0
    for bit in range(bits):
        out |= ((value >> bit) & 1) << (bits - 1 - bit)
    return out


def sin_cos(angle):
    turns = jnp.floor(angle * (2.0 / math.pi) + 0.5)
    rest = angle - turns * 1.5703125
    rest = rest - turns * 4.837512969970703125e-4
    rest = rest - turns * 7.54978995489188e-8
    square = rest * rest
    sine = -1.9515295891e-4 * square + 8.3321608736e-3
    sine = (sine * square - 1.6666654611e-1) * square * rest + rest
    cosine = 2.443315711809948e-5 * square - 1.388731625493765e-3
    cosine = (cosine * square + 4.166664568298827e-2) * square * square
    cosine = cosine - 0.5 * square + 1.0
    quadrant = turns.astype(jnp.int32) & 3
    swap = (quadrant & 1) == 1
    first = jnp.where(swap, cosine, sine)
    second = jnp.where(swap, sine, cosine)
    out_sine = jnp.where(quadrant >= 2, -first, first)
    out_cosine = jnp.where((quadrant == 1) | (quadrant == 2), -second, second)
    return out_sine, out_cosine


def exchange(words, bit, inner):
    blocks, sublanes, lanes = words[0].shape
    vregs = inner.bit_length() - 1
    if bit < vregs or bit >= vregs + 10:
        half = 1 << bit if bit < vregs else inner
        shape = (blocks // (2 * half), 2, half, sublanes, lanes)
        parts = [word.reshape(shape) for word in words]
        lower = [part[:, 0] for part in parts]
        upper = [part[:, 1] for part in parts]
        swap = lower[0] > upper[0]
        out = []
        for a, b in zip(lower, upper):
            first = jnp.where(swap, b, a)
            second = jnp.where(swap, a, b)
            out.append(jnp.stack([first, second], axis=1).reshape(blocks, sublanes, lanes))
        return out
    axis = 1 if bit < vregs + 3 else 2
    step = 1 << (bit - vregs) if axis == 1 else 1 << (bit - vregs - 3)
    size = (sublanes, lanes)[axis - 1]
    spots = lax.broadcasted_iota(jnp.int32, (1, sublanes, lanes), axis)
    high = jnp.broadcast_to((spots & step) != 0, words[0].shape)
    sign = jnp.where((spots & step) != 0, -1.0, 1.0)
    partners = []
    for word in words:
        back = pltpu.roll(word, step, axis)
        if 2 * step == size:
            partners.append(back)
        else:
            partners.append(jnp.where(high, back, pltpu.roll(word, size - step, axis)))
    take = (partners[0] - words[0]) * sign < 0.0
    return [jnp.where(take, partner, word) for partner, word in zip(partners, words)]


def order_bit(shape, bit):
    vregs = shape[0].bit_length() - 1
    if bit < vregs:
        return lax.broadcasted_iota(jnp.int32, shape, 0) & (1 << bit)
    if bit < vregs + 3:
        return lax.broadcasted_iota(jnp.int32, shape, 1) & (1 << (bit - vregs))
    return lax.broadcasted_iota(jnp.int32, shape, 2) & (1 << (bit - vregs - 3))


def order_of(shape):
    block = lax.broadcasted_iota(jnp.int32, shape, 0)
    row = lax.broadcasted_iota(jnp.int32, shape, 1)
    lane = lax.broadcasted_iota(jnp.int32, shape, 2)
    return (lane * shape[1] + row) * shape[0] + block


def sort_words(words):
    shape = words[0].shape
    bits = math.prod(shape).bit_length() - 1
    key, rest = words[0], list(words[1:])
    sign = None
    for phase in range(1, bits + 1):
        after = 1.0
        if phase < bits:
            after = jnp.where(order_bit(shape, phase) != 0, -1.0, 1.0)
        turn = after if sign is None else after * sign
        key = key * turn
        sign = after
        for bit in reversed(range(phase)):
            key, *rest = exchange([key] + rest, bit, shape[0])
    return [key] + rest


def tile_spans(tiles):
    if tiles % sum(SHARES):
        return [(0, tiles)]
    unit = tiles // sum(SHARES)
    return [(sum(SHARES[:g]) * unit, share * unit) for g, share in enumerate(SHARES)]


def apply_kernel(
    counts,
    count_ref,
    misfit_ref,
    look_ref,
    tile_ref,
    cell_ref,
    guess,
    visc,
    fric,
    base,
    slope,
    mask,
    adj_out,
    maps_out,
    *scratch,
):
    nx, ny, nz = counts
    bits = nz.bit_length() - 1
    tiles = nx * ny
    layers, rows, cols = visc.shape
    size = rows // nz
    spans = tile_spans(tiles)
    groups = len(spans)
    scratch = list(scratch)
    accs = [scratch.pop(0) for _ in range(bits)]
    recvs = [scratch.pop(0) for _ in range(bits)]
    (
        pixels,
        sums,
        lhs,
        rhs,
        acc,
        tile_in,
        block,
        forcing,
        middle,
        west_edge,
        east_edge,
        south_edge,
        north_edge,
        halo_w,
        halo_e,
        halo_s,
        halo_n,
        halo_se,
        halo_nw,
        halo_d,
        halo_u,
        visc_d,
        part,
        part_in,
        edge_w,
        edge_e,
        edge_s,
        edge_n,
        ring_w,
        ring_e,
        ring_s,
        ring_n,
        ring_se,
        ring_nw,
        late,
        late_in,
        half_sem,
        tile_sem,
        last_send,
        last_recv,
        halo_sem,
        visc_sem,
        part_sem,
        ring_send,
        ring_recv,
        late_sem,
    ) = scratch
    chunks, chunk_rows = pixels.shape[1] // tiles, pixels.shape[2]
    gx, gy, gz = lax.axis_index("gx"), lax.axis_index("gy"), lax.axis_index("gz")
    tile = gx * ny + gy
    lane_step = 16
    row_step = 8
    top = nz - 1

    def remote(src, dst, send, recv, device):
        return pltpu.make_async_remote_copy(
            src_ref=src,
            dst_ref=dst,
            send_sem=send,
            recv_sem=recv,
            device_id=device,
            device_id_type=pl.DeviceIdType.MESH,
        )

    barrier = pltpu.get_barrier_semaphore()
    layer_peers = [(gx, gy, lax.rem(gz + o, nz)) for o in range(1, nz)]
    tile_peers = []
    for o in range(1, tiles):
        other = lax.rem(tile + o, tiles)
        tile_peers.append((other, (lax.div(other, ny), lax.rem(other, ny), gz)))
    for device in layer_peers + [device for _, device in tile_peers]:
        pl.semaphore_signal(barrier, inc=1, device_id=device, device_id_type=pl.DeviceIdType.MESH)

    def prepare():
        sine, cosine = sin_cos(look_ref[...])
        order = lax.broadcasted_iota(jnp.int32, misfit_ref.shape, 0) * misfit_ref.shape[1]
        order = order + lax.broadcasted_iota(jnp.int32, misfit_ref.shape, 1)
        value = jnp.where(order < count_ref[0], misfit_ref[...], 0.0)
        total_rows, lanes = misfit_ref.shape
        cells = rows * cols
        cap = chunks * chunk_rows * lanes
        names = tile_ref[...]
        key = (names * cells + cell_ref[...]).astype(jnp.float32)
        shape = (total_rows // 8, 8, lanes)
        words = [word.reshape(shape) for word in (key, value * cosine, value * sine)]
        words = sort_words(words)
        place = total_rows * lanes - 1 - order_of(shape)
        filler = jnp.zeros(shape, jnp.float32)
        for t in range(tiles - 1):
            below = jnp.where(names <= t, 1.0, 0.0)
            below = jnp.sum(jnp.sum(below, axis=0, keepdims=True), axis=1, keepdims=True)
            spare = (float(cap * (t + 1)) - below).reshape(1, 1, 1)
            filler = filler + jnp.where(place.astype(jnp.float32) >= spare, float(cells), 0.0)
        zero = jnp.zeros(shape, jnp.float32)
        words = [jnp.concatenate(pair, axis=0) for pair in zip(words, (filler, zero, zero))]
        for bit in reversed(range((total_rows * lanes).bit_length())):
            words = exchange(words, bit, shape[0])
        width = chunk_rows
        for side in range(2):
            half = slice(side * shape[0], (side + 1) * shape[0])
            key, fx, fy = [word[half].reshape(total_rows, lanes).T for word in words]
            spots = lax.broadcasted_iota(jnp.int32, (lanes, total_rows), 0) + side * lanes
            owner = lax.div(spots * total_rows, cap).astype(jnp.float32)
            cell = key - owner * float(cells)
            row = jnp.floor((cell + 0.5) * (1.0 / cols))
            fields = []
            for f in (fx, fy):
                high = f.astype(jnp.bfloat16).astype(jnp.float32)
                fields += [high, f - high]
            fields += [row, cell - row * float(cols)]
            for f, field in enumerate(fields):
                for r in range(lanes // width):
                    pixels[f, side * (lanes // width) + r] = field[r * width : (r + 1) * width, :]

    starts = []
    length = nz // 2
    for bit in range(bits):
        own_bit = lax.rem(lax.div(gz, 1 << bit), 2)
        keep = own_bit * length
        give = (1 - own_bit) * length
        peer = (gx, gy, gz + (1 - 2 * own_bit) * (1 << bit))
        starts.append((keep, give, length, peer))
        length //= 2

    def half_copy(bit, g):
        _, give, length, peer = starts[bit]
        source = sums if bit == 0 else accs[bit - 1]
        own = pl.ds(*spans[g])
        return remote(
            source.at[pl.ds(give, length), own],
            recvs[bit].at[:, own],
            half_sem.at[0, bit, g],
            half_sem.at[1, bit, g],
            peer,
        )

    def bin_group(g):
        def build(i, slot):
            ids = lax.broadcasted_iota(jnp.int32, (cols, 128), 0)
            ids = ids.astype(jnp.float32).astype(jnp.bfloat16)
            row_ids = lax.broadcasted_iota(jnp.int32, (rows, 128), 0)
            row_ids = row_ids.astype(jnp.float32).astype(jnp.bfloat16)
            one = jnp.ones((cols, 128), jnp.bfloat16)
            none = jnp.zeros((cols, 128), jnp.bfloat16)
            zero = jnp.zeros((rows, 128), jnp.bfloat16)
            fields = [pixels[f, i] for f in range(6)]

            def spread(field, j, length):
                strip = jnp.broadcast_to(field[j : j + 1, :], (16, 128)).astype(jnp.bfloat16)
                return jnp.concatenate([strip] * (length // 16), axis=0)

            for j in range(chunk_rows):
                span = slice(j * 128, (j + 1) * 128)
                rhs[slot, :, span] = jnp.where(ids == spread(fields[5], j, cols), one, none)
                hit = row_ids == spread(fields[4], j, rows)
                for f in range(4):
                    start = ((f % 2) * 2 + f // 2) * rows
                    piece = spread(fields[f], j, rows)
                    lhs[slot, start : start + rows, span] = jnp.where(hit, piece, zero)

        def one_tile(n, carry):
            t = spans[g][0] + n
            for slot in range(chunks):
                build(t * chunks + slot, slot)
                product = lax.dot_general(
                    lhs[slot], rhs[slot], (((1,), (1,)), ((), ())), preferred_element_type=jnp.float32
                )
                if slot == 0:
                    acc[...] = product
                else:
                    acc[...] += product
            half = 2 * rows
            for c in range(2):
                for q in range(nz):
                    begin = c * rows + q * size
                    sums[reverse_bits(q, bits), t, c] = (
                        acc[begin : begin + size] + acc[half + begin : half + begin + size]
                    )
            return carry

        lax.fori_loop(0, spans[g][1], one_tile, 0)

    def pack(field):
        lanes = lax.broadcasted_iota(jnp.int32, (rows, 128), 1)
        west = jnp.zeros((rows, 128), jnp.float32)
        east = jnp.zeros((rows, 128), jnp.float32)
        for f in range(3):
            for k in range(layers):
                value = field[f, k] if f < 2 else visc[k]
                south_edge[f * row_step + k : f * row_step + k + 1, :] = value[0:1, :]
                north_edge[f * row_step + k : f * row_step + k + 1, :] = value[rows - 1 : rows, :]
                lane = lanes == f * lane_step + k
                west = jnp.where(lane, lane_column(value, 0, west), west)
                east = jnp.where(lane, lane_column(value, cols - 1, east), east)
        west_edge[...] = west
        east_edge[...] = east

    def halo_copies(field, turn):
        def one(index, src, dst, device):
            return remote(src, dst, halo_sem.at[turn, 0, index], halo_sem.at[turn, 1, index], device)

        return [
            (one(0, west_edge, halo_e.at[turn], (gx - 1, gy, gz)), gx > 0, gx < nx - 1),
            (one(1, east_edge, halo_w.at[turn], (gx + 1, gy, gz)), gx < nx - 1, gx > 0),
            (one(2, south_edge, halo_n.at[turn], (gx, gy - 1, gz)), gy > 0, gy < ny - 1),
            (one(3, north_edge, halo_s.at[turn], (gx, gy + 1, gz)), gy < ny - 1, gy > 0),
            (
                one(4, north_edge.at[:, 0:128], halo_se.at[turn], (gx - 1, gy + 1, gz)),
                (gx > 0) & (gy < ny - 1),
                (gx < nx - 1) & (gy > 0),
            ),
            (
                one(5, east_edge.at[0:8, :], halo_nw.at[turn], (gx + 1, gy - 1, gz)),
                (gx < nx - 1) & (gy > 0),
                (gx > 0) & (gy < ny - 1),
            ),
            (one(6, field.at[:, 0], halo_u.at[turn], (gx, gy, gz - 1)), gz > 0, gz < nz - 1),
            (one(7, field.at[:, layers - 1], halo_d.at[turn], (gx, gy, gz + 1)), gz < nz - 1, gz > 0),
        ]

    def start_all(copies):
        for copy, sends, _ in copies:

            @pl.when(sends)
            def _(copy=copy):
                copy.start()

    def wait_receives(copies):
        for copy, _, receives in copies:

            @pl.when(receives)
            def _(copy=copy):
                copy.wait_recv()

    def wait_sends(copies):
        for copy, sends, _ in copies:

            @pl.when(sends)
            def _(copy=copy):
                copy.wait_send()

    lane_ids = lax.broadcasted_iota(jnp.int32, (rows, cols), 1)
    row_ids = lax.broadcasted_iota(jnp.int32, (rows, cols), 0)

    def masks():
        mx = jnp.where((lane_ids < cols - 1) | (gx < nx - 1), 1.0, 0.0)
        my = jnp.where((row_ids < rows - 1) | (gy < ny - 1), 1.0, 0.0)
        return mx, my

    west_on = jnp.where(gx > 0, 1.0, 0.0)
    south_on = jnp.where(gy > 0, 1.0, 0.0)
    up_on = jnp.where(gz < nz - 1, 1.0, 0.0)

    def damping_of(k):
        scale = 18.0 * visc[k]
        if k == 0:
            scale = scale + jnp.where(gz == 0, fric[...], 0.0)
        return 0.6 / scale

    def west_stress(a, b, v, corner_a, corner_b, own_a, own_b, my_col):
        na = (from_north(a, corner_a) - a) * my_col
        nb = (from_north(b, corner_b) - b) * my_col
        ea = (own_a - a) * west_on
        eb = (own_b - b) * west_on
        return v * (4.0 * ea + 2.0 * nb) * west_on, v * (na + eb) * west_on

    def south_stress(a, b, v, corner_a, corner_b, own_a, own_b, mx_row):
        ea = (from_east(a, corner_a) - a) * mx_row
        eb = (from_east(b, corner_b) - b) * mx_row
        na = (own_a - a) * south_on
        nb = (own_b - b) * south_on
        return v * (4.0 * nb + 2.0 * ea) * south_on, v * (na + eb) * south_on

    def plane_image(va, vb, v, east_a, east_b, north_a, north_b, col_p, col_s, row_q, row_s, mx, my):
        ea = (from_east(va, east_a) - va) * mx
        eb = (from_east(vb, east_b) - vb) * mx
        na = (from_north(va, north_a) - va) * my
        nb = (from_north(vb, north_b) - vb) * my
        p = mx * v * (4.0 * ea + 2.0 * nb)
        q = my * v * (4.0 * nb + 2.0 * ea)
        s = v * (na + eb)
        sx = mx * s
        sy = my * s
        image_a = (from_west(p, col_p) - p) + (from_south(sy, row_s) - sy)
        image_b = (from_south(q, row_q) - q) + (from_west(sx, col_s) - sx)
        return image_a, image_b

    def sweep(field, turn, store):
        mx, my = masks()
        my_col = my[:, 0:128]
        mx_row = mx[0:8, :]
        west = jnp.where(gx > 0, halo_w[turn], 0.0)
        east = jnp.where(gx < nx - 1, halo_e[turn], 0.0)
        south = jnp.where(gy > 0, halo_s[turn], 0.0)
        north = jnp.where(gy < ny - 1, halo_n[turn], 0.0)
        corner_se = jnp.where((gx < nx - 1) & (gy > 0), halo_se[turn], 0.0)
        corner_nw = jnp.where((gx > 0) & (gy < ny - 1), halo_nw[turn], 0.0)
        own_w = west_edge[...]
        own_s = south_edge[...]
        corner_b = pltpu.roll(corner_nw, 128 - lane_step, 1)
        col_p, col_s = west_stress(
            west,
            pltpu.roll(west, 128 - lane_step, 1),
            pltpu.roll(west, 128 - 2 * lane_step, 1),
            corner_nw[0:1, :],
            corner_b[0:1, :],
            own_w,
            pltpu.roll(own_w, 128 - lane_step, 1),
            my_col,
        )
        south_a, south_b, south_v = south[0:8], south[8:16], south[16:24]
        row_q, row_s = south_stress(
            south_a,
            south_b,
            south_v,
            lane_column(corner_se[0:8], 0, south_a),
            lane_column(corner_se[8:16], 0, south_b),
            own_s[0:8],
            own_s[8:16],
            mx_row,
        )

        below_v = jnp.where(gz > 0, visc_d[...], 0.0)
        low_a = 4.0 * below_v * (field[0, 0] - jnp.where(gz > 0, halo_d[turn, 0], 0.0))
        low_b = 4.0 * below_v * (field[1, 0] - jnp.where(gz > 0, halo_d[turn, 1], 0.0))
        for k in range(layers):
            va, vb, v = field[0, k], field[1, k], visc[k]
            if k < layers - 1:
                top_a = 4.0 * v * (field[0, k + 1] - va)
                top_b = 4.0 * v * (field[1, k + 1] - vb)
            else:
                top_a = 4.0 * v * (jnp.where(gz < nz - 1, halo_u[turn, 0], 0.0) - va) * up_on
                top_b = 4.0 * v * (jnp.where(gz < nz - 1, halo_u[turn, 1], 0.0) - vb) * up_on
            image_a, image_b = plane_image(
                va,
                vb,
                v,
                lane_column(east, k, va),
                lane_column(east, lane_step + k, vb),
                north[k : k + 1],
                north[row_step + k : row_step + k + 1],
                lane_column(col_p, k, va),
                lane_column(col_s, k, va),
                row_q[k : k + 1],
                row_s[k : k + 1],
                mx,
                my,
            )
            image_a = image_a + (low_a - top_a)
            image_b = image_b + (low_b - top_b)
            if k == 0:
                basal = jnp.where(gz == 0, fric[...], 0.0)
                image_a = image_a + basal * va
                image_b = image_b + basal * vb
            low_a, low_b = top_a, top_b
            damp = damping_of(k)
            store(k, va - damp * image_a, vb - damp * image_b)

    def store_first(k, new_a, new_b):
        middle[0, k] = new_a
        middle[1, k] = new_b

    def store_second(k, new_a, new_b):
        adj_out[0, k] = new_a
        adj_out[1, k] = new_b
        term = slope[0] * new_a + slope[1] * new_b
        if k == 0:
            on_base = jnp.where(gz == 0, 1.0, 0.0)
            land = mask[...].astype(jnp.float32)
            part[0] = -on_base * land * fric[...] * (base[0] * new_a + base[1] * new_b)
            part[1] = term
        elif k < layers - 1:
            part[1] = part[1] + term
        else:
            part[1] = 0.25 * mask[...].astype(jnp.float32) * (part[1] + term)

    def tile_copy(t):
        device = (t // ny, t % ny, gz)
        return remote(
            total.at[0, t], tile_in.at[tile], tile_sem.at[0, t], tile_sem.at[1, tile], device
        )

    def finish(bit, g):
        keep, give, length, _ = starts[bit]
        source = sums if bit == 0 else accs[bit - 1]
        own = pl.ds(*spans[g])
        half_copy(bit, g).wait_recv()
        if bit + 1 < bits:
            next_keep, next_give, next_length, _ = starts[bit + 1]
            for begin in (next_give, next_keep):
                accs[bit][pl.ds(begin, next_length), own] = (
                    source[pl.ds(keep + begin, next_length), own]
                    + recvs[bit][pl.ds(begin, next_length), own]
                )
                if begin is next_give:
                    half_copy(bit + 1, g).start()
            return
        accs[bit][:, own] = source[pl.ds(keep, length), own] + recvs[bit][:, own]
        for t in range(spans[g][0], sum(spans[g])):

            @pl.when(tile != t)
            def _(t=t):
                tile_copy(t).start()

            @pl.when(tile == t)
            def _(t=t):
                tile_in[t] = total[0, t]

    total = accs[bits - 1]

    def part_copy(o):
        device = layer_peers[o - 1]
        begin = pl.multiple_of(device[2] * size, size)
        return remote(
            part.at[:, pl.ds(begin, size), :],
            part_in.at[o - 1],
            part_sem.at[0, o - 1],
            part_sem.at[1, o - 1],
            device,
        )

    prepare()
    bin_group(0)
    pl.semaphore_wait(barrier, nz - 1 + tiles - 1)
    half_copy(0, 0).start()
    visc_up = (
        remote(visc.at[layers - 1], visc_d, visc_sem.at[0], visc_sem.at[1], (gx, gy, gz + 1)),
        gz < nz - 1,
        gz > 0,
    )
    pack(guess)
    first = halo_copies(guess, 0) + [visc_up]
    second = halo_copies(middle, 1)
    start_all(first)

    def early(turn):
        if turn == groups + FIRST:
            wait_receives(first)
            wait_sends(first)
            sweep(guess, 0, store_first)
            pack(middle)
            start_all(second)
        elif turn == groups + bits - 1:
            wait_receives(second)
            sweep(middle, 1, store_second)
            for o in range(1, nz):
                part_copy(o).start()
            wait_sends(second)

    for turn in range(1, groups + bits):
        if turn < groups:
            bin_group(turn)
            half_copy(0, turn).start()
        for bit in reversed(range(bits)):
            g = turn - 1 - bit
            if 0 <= g < groups:
                finish(bit, g)
        early(turn)
    for t in range(tiles):

        @pl.when(tile != t)
        def _(t=t):
            remote(
                total.at[0, t], tile_in.at[t], tile_sem.at[0, t], tile_sem.at[1, t], (t // ny, t % ny, gz)
            ).wait_recv()

    own_rows = pl.ds(pl.multiple_of(gz * size, size), size)
    value = tile_in[0]
    for t in range(1, tiles):
        value = value + tile_in[t]
    land = mask[own_rows, :].astype(jnp.float32)
    value = value * land[None]
    block[...] = value

    lanes = lax.broadcasted_iota(jnp.int32, (size, 128), 1)
    west = jnp.zeros((size, 128), jnp.float32)
    east = jnp.zeros((size, 128), jnp.float32)
    for c in range(2):
        west = jnp.where(lanes == c * lane_step, lane_column(value[c], 0, west), west)
        east = jnp.where(lanes == c * lane_step, lane_column(value[c], cols - 1, east), east)
        edge_s[c * row_step : c * row_step + 1, :] = value[c, 0:1, :]
        edge_n[c * row_step : c * row_step + 1, :] = value[c, size - 1 : size, :]
    edge_w[...] = west
    edge_e[...] = east

    is_top = gz == top
    low = gz == 0

    def ring_one(index, src, dst, slot, device):
        return remote(src, dst, ring_send.at[index], ring_recv.at[slot], device)

    def ring_column(index, src, ring, q, device, slot):
        return ring_one(index, src, ring.at[q], slot, device)

    ring_sends = [
        (ring_one(0, edge_w, ring_e.at[gz], gz, (gx - 1, gy, top)), gx > 0),
        (ring_one(1, edge_e, ring_w.at[gz], nz + gz, (gx + 1, gy, top)), gx < nx - 1),
        (ring_one(2, edge_s, ring_n, 2 * nz, (gx, gy - 1, top)), low & (gy > 0)),
        (ring_one(3, edge_n, ring_s, 2 * nz + 1, (gx, gy + 1, top)), is_top & (gy < ny - 1)),
        (
            ring_one(4, edge_n.at[:, 0:128], ring_se, 2 * nz + 2, (gx - 1, gy + 1, top)),
            is_top & (gx > 0) & (gy < ny - 1),
        ),
        (
            ring_one(5, edge_e.at[0:8, :], ring_nw, 2 * nz + 3, (gx + 1, gy - 1, top)),
            low & (gx < nx - 1) & (gy > 0),
        ),
    ]
    for copy, sends in ring_sends:

        @pl.when(sends)
        def _(copy=copy):
            copy.start()

    to_last = remote(block, forcing.at[gz], last_send, last_recv.at[gz], (gx, gy, top))

    @pl.when(gz < top)
    def _():
        to_last.start()

    def late_copy(j):
        return remote(late.at[j], late_in, late_sem.at[0, j], late_sem.at[1, 0], (gx, gy, j))

    @pl.when(is_top)
    def _():
        forcing[top] = block[...]
        for j in range(top):
            remote(block, forcing.at[j], last_send, last_recv.at[j], (gx, gy, 0)).wait_recv()
        peer = (lax.rem(gx + 1, nx), gy, top)
        for j in range(nz):

            @pl.when(gx < nx - 1)
            def _(j=j):
                ring_one(0, edge_w, ring_e.at[j], j, peer).wait_recv()

            @pl.when(gx > 0)
            def _(j=j):
                ring_one(1, edge_e, ring_w.at[j], nz + j, peer).wait_recv()

        @pl.when(gy < ny - 1)
        def _():
            ring_one(2, edge_s, ring_n, 2 * nz, peer).wait_recv()

        @pl.when(gy > 0)
        def _():
            ring_one(3, edge_n, ring_s, 2 * nz + 1, peer).wait_recv()

        @pl.when((gx < nx - 1) & (gy > 0))
        def _():
            ring_one(4, edge_n.at[:, 0:128], ring_se, 2 * nz + 2, peer).wait_recv()

        @pl.when((gx > 0) & (gy < ny - 1))
        def _():
            ring_one(5, edge_e.at[0:8, :], ring_nw, 2 * nz + 3, peer).wait_recv()

        mx, my = masks()
        my_col = my[:, 0:128]
        mx_row = mx[0:8, :]
        last = layers - 1
        shift = 128 - 2 * lane_step - last

        def scaled(on, force, v):
            return jnp.where(on, force * (0.6 / (18.0 * v)), 0.0)

        def columns(value):
            a = lane_column(value, 0, value)
            return a, lane_column(value, lane_step, value)

        v = visc[last]
        damp = damping_of(last)
        force_a = jnp.concatenate([forcing[q, 0] for q in range(nz)], axis=0)
        force_b = jnp.concatenate([forcing[q, 1] for q in range(nz)], axis=0)
        ea = damp * force_a
        eb = damp * force_b

        west_v = lane_column(halo_w[0], 2 * lane_step + last, halo_w[0])
        east_v = lane_column(halo_e[0], 2 * lane_step + last, halo_e[0])
        south_v = jnp.broadcast_to(halo_s[0, 16 + last : 17 + last, :], (8, cols))
        north_v = jnp.broadcast_to(halo_n[0, 16 + last : 17 + last, :], (8, cols))
        nw_v = lane_column(halo_nw[0], 2 * lane_step + last, halo_nw[0])
        se_v = jnp.broadcast_to(halo_se[0, 16 + last : 17 + last, :], (8, 128))

        ring_w_all = jnp.concatenate([ring_w[q] for q in range(nz)], axis=0)
        ring_e_all = jnp.concatenate([ring_e[q] for q in range(nz)], axis=0)
        west_a, west_b = [scaled(gx > 0, f, west_v) for f in columns(ring_w_all)]
        east_a, east_b = [scaled(gx < nx - 1, f, east_v) for f in columns(ring_e_all)]
        nw_on = (gx > 0) & (gy < ny - 1)
        se_on = (gx < nx - 1) & (gy > 0)
        nw_a, nw_b = [scaled(nw_on, f, nw_v) for f in columns(ring_nw[...])]
        south_a = scaled(gy > 0, ring_s[0:8], south_v)
        south_b = scaled(gy > 0, ring_s[8:16], south_v)
        north_a = scaled(gy < ny - 1, ring_n[0:8], north_v)
        north_b = scaled(gy < ny - 1, ring_n[8:16], north_v)
        se_a = scaled(se_on, ring_se[0:8], se_v)
        se_b = scaled(se_on, ring_se[8:16], se_v)
        west_v = jnp.where(gx > 0, west_v, 0.0)
        south_v = jnp.where(gy > 0, south_v, 0.0)

        col_p, col_s = west_stress(
            west_a,
            west_b,
            west_v,
            nw_a[0:1, :],
            nw_b[0:1, :],
            lane_column(ea, 0, west_a),
            lane_column(eb, 0, west_b),
            my_col,
        )
        row_q, row_s = south_stress(
            south_a,
            south_b,
            south_v,
            lane_column(se_a, 0, south_a),
            lane_column(se_b, 0, south_b),
            jnp.broadcast_to(ea[0:1, :], south_a.shape),
            jnp.broadcast_to(eb[0:1, :], south_b.shape),
            mx_row,
        )
        image_a, image_b = plane_image(
            ea,
            eb,
            v,
            lane_column(east_a, 0, ea),
            lane_column(east_b, 0, eb),
            north_a[0:1],
            north_b[0:1],
            lane_column(col_p, 0, ea),
            lane_column(col_s, 0, ea),
            row_q[0:1],
            row_s[0:1],
            mx,
            my,
        )
        below = 4.0 * visc[last - 1]
        image_a = image_a + below * ea
        image_b = image_b + below * eb
        top_a = ea + damp * (force_a - image_a)
        top_b = eb + damp * (force_b - image_b)
        lift = damping_of(last - 1) * below
        low_a = lift * ea
        low_b = lift * eb
        land = mask[...].astype(jnp.float32)
        drive = 0.25 * land * (slope[0] * (top_a + low_a) + slope[1] * (top_b + low_b))
        for j in range(nz):
            late[j] = drive[j * size : (j + 1) * size, :]
        for j in range(top):
            late_copy(j).start()
        adj_out[0, last] = adj_out[0, last] + top_a
        adj_out[1, last] = adj_out[1, last] + top_b
        adj_out[0, last - 1] = adj_out[0, last - 1] + low_a
        adj_out[1, last - 1] = adj_out[1, last - 1] + low_b
        for j in range(top):
            late_copy(j).wait_send()

    gathered = part[:, own_rows, :]
    for o in range(1, nz):
        part_copy(o).wait_recv()
        gathered = gathered + part_in[o - 1]
    maps_out[0] = gathered[0]

    @pl.when(is_top)
    def _():
        maps_out[1] = gathered[1] + late[top]

    @pl.when(gz < top)
    def _():
        remote(late.at[0], late_in, late_sem.at[0, 0], late_sem.at[1, 0], (gx, gy, top)).wait_recv()
        maps_out[1] = gathered[1] + late_in[...]

    for bit in range(bits):
        for g in range(groups):
            half_copy(bit, g).wait_send()
    for t in range(tiles):

        @pl.when(tile != t)
        def _(t=t):
            tile_copy(t).wait_send()

    @pl.when(gz < top)
    def _():
        to_last.wait_send()

    for copy, sends in ring_sends:

        @pl.when(sends)
        def _(copy=copy):
            copy.wait_send()

    for o in range(1, nz):
        part_copy(o).wait_send()


def apply_twice(count, pixels, guess, visc, fric, base, slope, mask, counts):
    nx, ny, nz = counts
    tiles = nx * ny
    bits = nz.bit_length() - 1
    _, layers, rows, cols = guess.shape
    size = rows // nz
    f32 = jnp.float32
    groups = len(tile_spans(tiles))
    per_device = pixels[0].shape[0]
    cap = 2 * per_device // tiles
    chunk_rows = min(8, cap // 128)
    depth = chunk_rows * 128
    chunks = cap // depth
    flat = [value.reshape(per_device // 128, 128) for value in pixels]
    halves = [pltpu.VMEM((nz >> (bit + 1), tiles, 2, size, cols), f32) for bit in range(bits)]
    vmem = pl.BlockSpec(memory_space=pltpu.VMEM)
    dma = pltpu.SemaphoreType.DMA
    return pl.pallas_call(
        functools.partial(apply_kernel, counts),
        in_specs=[pl.BlockSpec(memory_space=pltpu.SMEM)] + [vmem] * 10,
        out_specs=(vmem, vmem),
        out_shape=(pltpu.VMEM(guess.shape, f32), pltpu.VMEM((2, size, cols), f32)),
        scratch_shapes=halves
        + halves
        + [
            pltpu.VMEM((6, tiles * chunks, chunk_rows, 128), f32),
            pltpu.VMEM((nz, tiles, 2, size, cols), f32),
            pltpu.VMEM((chunks, 4 * rows, depth), jnp.bfloat16),
            pltpu.VMEM((chunks, cols, depth), jnp.bfloat16),
            pltpu.VMEM((4 * rows, cols), f32),
            pltpu.VMEM((tiles, 2, size, cols), f32),
            pltpu.VMEM((2, size, cols), f32),
            pltpu.VMEM((nz, 2, size, cols), f32),
            pltpu.VMEM(guess.shape, f32),
            pltpu.VMEM((rows, 128), f32),
            pltpu.VMEM((rows, 128), f32),
            pltpu.VMEM((24, cols), f32),
            pltpu.VMEM((24, cols), f32),
            pltpu.VMEM((2, rows, 128), f32),
            pltpu.VMEM((2, rows, 128), f32),
            pltpu.VMEM((2, 24, cols), f32),
            pltpu.VMEM((2, 24, cols), f32),
            pltpu.VMEM((2, 24, 128), f32),
            pltpu.VMEM((2, 8, 128), f32),
            pltpu.VMEM((2, 2, rows, cols), f32),
            pltpu.VMEM((2, 2, rows, cols), f32),
            pltpu.VMEM((rows, cols), f32),
            pltpu.VMEM((2, rows, cols), f32),
            pltpu.VMEM((nz - 1, 2, size, cols), f32),
            pltpu.VMEM((size, 128), f32),
            pltpu.VMEM((size, 128), f32),
            pltpu.VMEM((16, cols), f32),
            pltpu.VMEM((16, cols), f32),
            pltpu.VMEM((nz, size, 128), f32),
            pltpu.VMEM((nz, size, 128), f32),
            pltpu.VMEM((16, cols), f32),
            pltpu.VMEM((16, cols), f32),
            pltpu.VMEM((16, 128), f32),
            pltpu.VMEM((8, 128), f32),
            pltpu.VMEM((nz, size, cols), f32),
            pltpu.VMEM((size, cols), f32),
            dma((2, bits, groups)),
            dma((2, tiles)),
            dma,
            dma((nz,)),
            dma((2, 2, 8)),
            dma((2,)),
            dma((2, nz - 1)),
            dma((6,)),
            dma((2 * nz + 4,)),
            dma((2, nz)),
        ],
        compiler_params=pltpu.CompilerParams(
            collective_id=0, has_side_effects=True, vmem_limit_bytes=56 * 2**20
        ),
        name="apply_twice",
    )(count, *flat, guess, visc, fric, base, slope, mask)


def body(
    adjoint_guess,
    viscosity,
    friction,
    base_velocity,
    surface_slope,
    ice_mask,
    pixel_misfit,
    pixel_look,
    pixel_tile,
    pixel_cell,
    pixel_count,
):
    sizes = tuple(lax.axis_size(name) for name in ("gx", "gy", "gz"))
    pixels = (pixel_misfit, pixel_look, pixel_tile[:, 0], pixel_cell)
    return apply_twice(
        pixel_count,
        pixels,
        adjoint_guess,
        viscosity,
        friction,
        base_velocity,
        surface_slope,
        ice_mask,
        sizes,
    )


def solution(mesh):
    return jax.shard_map(
        body,
        mesh=mesh,
        in_specs=(
            P(None, "gz", "gy", "gx"),
            P("gz", "gy", "gx"),
            P("gy", "gx"),
            P(None, "gy", "gx"),
            P(None, "gy", "gx"),
            P("gy", "gx"),
            P(("gx", "gy", "gz")),
            P(("gx", "gy", "gz")),
            P(("gx", "gy", "gz"), None),
            P(("gx", "gy", "gz")),
            P(("gx", "gy", "gz")),
        ),
        out_specs=(P(None, "gz", "gy", "gx"), P(None, ("gy", "gz"), "gx")),
        check_vma=False,
    )
```

```python
import functools
import math

import jax
import jax.numpy as jnp
from jax import lax
from jax.experimental import pallas as pl
from jax.experimental.pallas import tpu as pltpu
from jax.sharding import PartitionSpec as P

SHARES = (2, 2, 2, 2)
EARLY = (3, 6)
LAG = 2


def lane_column(pack, lane, like):
    return jnp.broadcast_to(pack[:, lane : lane + 1], like.shape)


def from_east(value, column):
    size = value.shape[1]
    lanes = lax.broadcasted_iota(jnp.int32, value.shape, 1)
    return jnp.where(lanes == size - 1, column, pltpu.roll(value, size - 1, 1))


def from_west(value, column):
    lanes = lax.broadcasted_iota(jnp.int32, value.shape, 1)
    return jnp.where(lanes == 0, column, pltpu.roll(value, 1, 1))


def from_north(value, row):
    size = value.shape[0]
    rows = lax.broadcasted_iota(jnp.int32, value.shape, 0)
    return jnp.where(rows == size - 1, row, pltpu.roll(value, size - 1, 0))


def from_south(value, row):
    rows = lax.broadcasted_iota(jnp.int32, value.shape, 0)
    return jnp.where(rows == 0, row, pltpu.roll(value, 1, 0))


def reverse_bits(value, bits):
    out = 0
    for bit in range(bits):
        out |= ((value >> bit) & 1) << (bits - 1 - bit)
    return out


def sin_cos(angle):
    turns = jnp.floor(angle * (2.0 / math.pi) + 0.5)
    rest = angle - turns * 1.5703125
    rest = rest - turns * 4.837512969970703125e-4
    rest = rest - turns * 7.54978995489188e-8
    square = rest * rest
    sine = -1.9515295891e-4 * square + 8.3321608736e-3
    sine = (sine * square - 1.6666654611e-1) * square * rest + rest
    cosine = 2.443315711809948e-5 * square - 1.388731625493765e-3
    cosine = (cosine * square + 4.166664568298827e-2) * square * square
    cosine = cosine - 0.5 * square + 1.0
    quadrant = turns.astype(jnp.int32) & 3
    swap = (quadrant & 1) == 1
    first = jnp.where(swap, cosine, sine)
    second = jnp.where(swap, sine, cosine)
    out_sine = jnp.where(quadrant >= 2, -first, first)
    out_cosine = jnp.where((quadrant == 1) | (quadrant == 2), -second, second)
    return out_sine, out_cosine


def exchange(words, bit, inner):
    blocks, sublanes, lanes = words[0].shape
    vregs = inner.bit_length() - 1
    if bit < vregs or bit >= vregs + 10:
        half = 1 << bit if bit < vregs else inner
        shape = (blocks // (2 * half), 2, half, sublanes, lanes)
        parts = [word.reshape(shape) for word in words]
        lower = [part[:, 0] for part in parts]
        upper = [part[:, 1] for part in parts]
        swap = lower[0] > upper[0]
        out = []
        for a, b in zip(lower, upper):
            first = jnp.where(swap, b, a)
            second = jnp.where(swap, a, b)
            out.append(jnp.stack([first, second], axis=1).reshape(blocks, sublanes, lanes))
        return out
    axis = 1 if bit < vregs + 3 else 2
    step = 1 << (bit - vregs) if axis == 1 else 1 << (bit - vregs - 3)
    size = (sublanes, lanes)[axis - 1]
    spots = lax.broadcasted_iota(jnp.int32, (1, sublanes, lanes), axis)
    high = jnp.broadcast_to((spots & step) != 0, words[0].shape)
    sign = jnp.where((spots & step) != 0, -1.0, 1.0)
    partners = []
    for word in words:
        back = pltpu.roll(word, step, axis)
        if 2 * step == size:
            partners.append(back)
        else:
            partners.append(jnp.where(high, back, pltpu.roll(word, size - step, axis)))
    take = (partners[0] - words[0]) * sign < 0.0
    return [jnp.where(take, partner, word) for partner, word in zip(partners, words)]


def order_bit(shape, bit):
    vregs = shape[0].bit_length() - 1
    if bit < vregs:
        return lax.broadcasted_iota(jnp.int32, shape, 0) & (1 << bit)
    if bit < vregs + 3:
        return lax.broadcasted_iota(jnp.int32, shape, 1) & (1 << (bit - vregs))
    return lax.broadcasted_iota(jnp.int32, shape, 2) & (1 << (bit - vregs - 3))


def order_of(shape):
    block = lax.broadcasted_iota(jnp.int32, shape, 0)
    row = lax.broadcasted_iota(jnp.int32, shape, 1)
    lane = lax.broadcasted_iota(jnp.int32, shape, 2)
    return (lane * shape[1] + row) * shape[0] + block


def sort_words(words):
    shape = words[0].shape
    bits = math.prod(shape).bit_length() - 1
    key, rest = words[0], list(words[1:])
    sign = None
    for phase in range(1, bits + 1):
        after = 1.0
        if phase < bits:
            after = jnp.where(order_bit(shape, phase) != 0, -1.0, 1.0)
        turn = after if sign is None else after * sign
        key = key * turn
        sign = after
        for bit in reversed(range(phase)):
            key, *rest = exchange([key] + rest, bit, shape[0])
    return [key] + rest


def tile_spans(tiles):
    if tiles % sum(SHARES):
        return [(0, tiles)]
    unit = tiles // sum(SHARES)
    return [(sum(SHARES[:g]) * unit, share * unit) for g, share in enumerate(SHARES)]


def apply_kernel(
    counts,
    count_ref,
    misfit_ref,
    look_ref,
    tile_ref,
    cell_ref,
    guess,
    visc,
    fric,
    base,
    slope,
    mask,
    adj_out,
    maps_out,
    *scratch,
):
    nx, ny, nz = counts
    bits = nz.bit_length() - 1
    tiles = nx * ny
    layers, rows, cols = visc.shape
    size = rows // nz
    spans = tile_spans(tiles)
    groups = len(spans)
    scratch = list(scratch)
    accs = [scratch.pop(0) for _ in range(bits)]
    recvs = [scratch.pop(0) for _ in range(bits)]
    (
        pixels,
        sums,
        lhs,
        rhs,
        acc,
        tile_in,
        block,
        forcing,
        middle,
        west_edge,
        east_edge,
        south_edge,
        north_edge,
        halo_w,
        halo_e,
        halo_s,
        halo_n,
        halo_se,
        halo_nw,
        halo_d,
        halo_u,
        visc_d,
        part,
        part_in,
        edge_w,
        edge_e,
        edge_s,
        edge_n,
        ring_w,
        ring_e,
        ring_s,
        ring_n,
        ring_se,
        ring_nw,
        late,
        late_in,
        half_sem,
        tile_sem,
        last_send,
        last_recv,
        halo_sem,
        visc_sem,
        part_sem,
        ring_send,
        ring_recv,
        late_sem,
    ) = scratch
    chunks, chunk_rows = pixels.shape[1] // tiles, pixels.shape[2]
    gx, gy, gz = lax.axis_index("gx"), lax.axis_index("gy"), lax.axis_index("gz")
    tile = gx * ny + gy
    lane_step = 16
    row_step = 8
    top = nz - 1

    def remote(src, dst, send, recv, device):
        return pltpu.make_async_remote_copy(
            src_ref=src,
            dst_ref=dst,
            send_sem=send,
            recv_sem=recv,
            device_id=device,
            device_id_type=pl.DeviceIdType.MESH,
        )

    barrier = pltpu.get_barrier_semaphore()
    layer_peers = [(gx, gy, lax.rem(gz + o, nz)) for o in range(1, nz)]
    tile_peers = []
    for o in range(1, tiles):
        other = lax.rem(tile + o, tiles)
        tile_peers.append((other, (lax.div(other, ny), lax.rem(other, ny), gz)))
    for device in layer_peers + [device for _, device in tile_peers]:
        pl.semaphore_signal(barrier, inc=1, device_id=device, device_id_type=pl.DeviceIdType.MESH)

    def prepare():
        sine, cosine = sin_cos(look_ref[...])
        order = lax.broadcasted_iota(jnp.int32, misfit_ref.shape, 0) * misfit_ref.shape[1]
        order = order + lax.broadcasted_iota(jnp.int32, misfit_ref.shape, 1)
        value = jnp.where(order < count_ref[0], misfit_ref[...], 0.0)
        total_rows, lanes = misfit_ref.shape
        cells = rows * cols
        cap = chunks * chunk_rows * lanes
        names = tile_ref[...]
        key = (names * cells + cell_ref[...]).astype(jnp.float32)
        shape = (total_rows // 8, 8, lanes)
        words = [word.reshape(shape) for word in (key, value * cosine, value * sine)]
        words = sort_words(words)
        place = total_rows * lanes - 1 - order_of(shape)
        filler = jnp.zeros(shape, jnp.float32)
        for t in range(tiles - 1):
            below = jnp.where(names <= t, 1.0, 0.0)
            below = jnp.sum(jnp.sum(below, axis=0, keepdims=True), axis=1, keepdims=True)
            spare = (float(cap * (t + 1)) - below).reshape(1, 1, 1)
            filler = filler + jnp.where(place.astype(jnp.float32) >= spare, float(cells), 0.0)
        zero = jnp.zeros(shape, jnp.float32)
        words = [jnp.concatenate(pair, axis=0) for pair in zip(words, (filler, zero, zero))]
        for bit in reversed(range((total_rows * lanes).bit_length())):
            words = exchange(words, bit, shape[0])
        width = chunk_rows
        for side in range(2):
            half = slice(side * shape[0], (side + 1) * shape[0])
            key, fx, fy = [word[half].reshape(total_rows, lanes).T for word in words]
            spots = lax.broadcasted_iota(jnp.int32, (lanes, total_rows), 0) + side * lanes
            owner = lax.div(spots * total_rows, cap).astype(jnp.float32)
            cell = key - owner * float(cells)
            row = jnp.floor((cell + 0.5) * (1.0 / cols))
            fields = []
            for f in (fx, fy):
                high = f.astype(jnp.bfloat16).astype(jnp.float32)
                fields += [high, f - high]
            fields += [row, cell - row * float(cols)]
            for f, field in enumerate(fields):
                for r in range(lanes // width):
                    pixels[f, side * (lanes // width) + r] = field[r * width : (r + 1) * width, :]

    starts = []
    length = nz // 2
    for bit in range(bits):
        own_bit = lax.rem(lax.div(gz, 1 << bit), 2)
        keep = own_bit * length
        give = (1 - own_bit) * length
        peer = (gx, gy, gz + (1 - 2 * own_bit) * (1 << bit))
        starts.append((keep, give, length, peer))
        length //= 2

    def half_copy(bit, g):
        _, give, length, peer = starts[bit]
        source = sums if bit == 0 else accs[bit - 1]
        own = pl.ds(*spans[g])
        return remote(
            source.at[pl.ds(give, length), own],
            recvs[bit].at[:, own],
            half_sem.at[0, bit, g],
            half_sem.at[1, bit, g],
            peer,
        )

    def bin_group(g):
        def build(i, slot):
            ids = lax.broadcasted_iota(jnp.int32, (cols, 128), 0)
            ids = ids.astype(jnp.float32).astype(jnp.bfloat16)
            row_ids = lax.broadcasted_iota(jnp.int32, (rows, 128), 0)
            row_ids = row_ids.astype(jnp.float32).astype(jnp.bfloat16)
            one = jnp.ones((cols, 128), jnp.bfloat16)
            none = jnp.zeros((cols, 128), jnp.bfloat16)
            zero = jnp.zeros((rows, 128), jnp.bfloat16)
            fields = [pixels[f, i] for f in range(6)]

            def spread(field, j, length):
                strip = jnp.broadcast_to(field[j : j + 1, :], (16, 128)).astype(jnp.bfloat16)
                return jnp.concatenate([strip] * (length // 16), axis=0)

            for j in range(chunk_rows):
                span = slice(j * 128, (j + 1) * 128)
                rhs[slot, :, span] = jnp.where(ids == spread(fields[5], j, cols), one, none)
                hit = row_ids == spread(fields[4], j, rows)
                for f in range(4):
                    start = ((f % 2) * 2 + f // 2) * rows
                    piece = spread(fields[f], j, rows)
                    lhs[slot, start : start + rows, span] = jnp.where(hit, piece, zero)

        def one_tile(n, carry):
            t = spans[g][0] + n
            for slot in range(chunks):
                build(t * chunks + slot, slot)
                product = lax.dot_general(
                    lhs[slot], rhs[slot], (((1,), (1,)), ((), ())), preferred_element_type=jnp.float32
                )
                if slot == 0:
                    acc[...] = product
                else:
                    acc[...] += product
            half = 2 * rows
            for c in range(2):
                for q in range(nz):
                    begin = c * rows + q * size
                    sums[reverse_bits(q, bits), t, c] = (
                        acc[begin : begin + size] + acc[half + begin : half + begin + size]
                    )
            return carry

        lax.fori_loop(0, spans[g][1], one_tile, 0)

    def pack(field):
        lanes = lax.broadcasted_iota(jnp.int32, (rows, 128), 1)
        west = jnp.zeros((rows, 128), jnp.float32)
        east = jnp.zeros((rows, 128), jnp.float32)
        for f in range(3):
            for k in range(layers):
                value = field[f, k] if f < 2 else visc[k]
                south_edge[f * row_step + k : f * row_step + k + 1, :] = value[0:1, :]
                north_edge[f * row_step + k : f * row_step + k + 1, :] = value[rows - 1 : rows, :]
                lane = lanes == f * lane_step + k
                west = jnp.where(lane, lane_column(value, 0, west), west)
                east = jnp.where(lane, lane_column(value, cols - 1, east), east)
        west_edge[...] = west
        east_edge[...] = east

    def halo_copies(field, turn):
        def one(index, src, dst, device):
            return remote(src, dst, halo_sem.at[turn, 0, index], halo_sem.at[turn, 1, index], device)

        return [
            (one(0, west_edge, halo_e.at[turn], (gx - 1, gy, gz)), gx > 0, gx < nx - 1),
            (one(1, east_edge, halo_w.at[turn], (gx + 1, gy, gz)), gx < nx - 1, gx > 0),
            (one(2, south_edge, halo_n.at[turn], (gx, gy - 1, gz)), gy > 0, gy < ny - 1),
            (one(3, north_edge, halo_s.at[turn], (gx, gy + 1, gz)), gy < ny - 1, gy > 0),
            (
                one(4, north_edge.at[:, 0:128], halo_se.at[turn], (gx - 1, gy + 1, gz)),
                (gx > 0) & (gy < ny - 1),
                (gx < nx - 1) & (gy > 0),
            ),
            (
                one(5, east_edge.at[0:8, :], halo_nw.at[turn], (gx + 1, gy - 1, gz)),
                (gx < nx - 1) & (gy > 0),
                (gx > 0) & (gy < ny - 1),
            ),
            (one(6, field.at[:, 0], halo_u.at[turn], (gx, gy, gz - 1)), gz > 0, gz < nz - 1),
            (one(7, field.at[:, layers - 1], halo_d.at[turn], (gx, gy, gz + 1)), gz < nz - 1, gz > 0),
        ]

    def start_all(copies):
        for copy, sends, _ in copies:

            @pl.when(sends)
            def _(copy=copy):
                copy.start()

    def wait_receives(copies):
        for copy, _, receives in copies:

            @pl.when(receives)
            def _(copy=copy):
                copy.wait_recv()

    def wait_sends(copies):
        for copy, sends, _ in copies:

            @pl.when(sends)
            def _(copy=copy):
                copy.wait_send()

    lane_ids = lax.broadcasted_iota(jnp.int32, (rows, cols), 1)
    row_ids = lax.broadcasted_iota(jnp.int32, (rows, cols), 0)

    def masks():
        mx = jnp.where((lane_ids < cols - 1) | (gx < nx - 1), 1.0, 0.0)
        my = jnp.where((row_ids < rows - 1) | (gy < ny - 1), 1.0, 0.0)
        return mx, my

    west_on = jnp.where(gx > 0, 1.0, 0.0)
    south_on = jnp.where(gy > 0, 1.0, 0.0)
    up_on = jnp.where(gz < nz - 1, 1.0, 0.0)

    def damping_of(k):
        scale = 18.0 * visc[k]
        if k == 0:
            scale = scale + jnp.where(gz == 0, fric[...], 0.0)
        return 0.6 / scale

    def west_stress(a, b, v, corner_a, corner_b, own_a, own_b, my_col):
        na = (from_north(a, corner_a) - a) * my_col
        nb = (from_north(b, corner_b) - b) * my_col
        ea = (own_a - a) * west_on
        eb = (own_b - b) * west_on
        return v * (4.0 * ea + 2.0 * nb) * west_on, v * (na + eb) * west_on

    def south_stress(a, b, v, corner_a, corner_b, own_a, own_b, mx_row):
        ea = (from_east(a, corner_a) - a) * mx_row
        eb = (from_east(b, corner_b) - b) * mx_row
        na = (own_a - a) * south_on
        nb = (own_b - b) * south_on
        return v * (4.0 * nb + 2.0 * ea) * south_on, v * (na + eb) * south_on

    def plane_image(va, vb, v, east_a, east_b, north_a, north_b, col_p, col_s, row_q, row_s, mx, my):
        ea = (from_east(va, east_a) - va) * mx
        eb = (from_east(vb, east_b) - vb) * mx
        na = (from_north(va, north_a) - va) * my
        nb = (from_north(vb, north_b) - vb) * my
        p = mx * v * (4.0 * ea + 2.0 * nb)
        q = my * v * (4.0 * nb + 2.0 * ea)
        s = v * (na + eb)
        sx = mx * s
        sy = my * s
        image_a = (from_west(p, col_p) - p) + (from_south(sy, row_s) - sy)
        image_b = (from_south(q, row_q) - q) + (from_west(sx, col_s) - sx)
        return image_a, image_b

    def sweep(field, turn, store):
        mx, my = masks()
        my_col = my[:, 0:128]
        mx_row = mx[0:8, :]
        west = jnp.where(gx > 0, halo_w[turn], 0.0)
        east = jnp.where(gx < nx - 1, halo_e[turn], 0.0)
        south = jnp.where(gy > 0, halo_s[turn], 0.0)
        north = jnp.where(gy < ny - 1, halo_n[turn], 0.0)
        corner_se = jnp.where((gx < nx - 1) & (gy > 0), halo_se[turn], 0.0)
        corner_nw = jnp.where((gx > 0) & (gy < ny - 1), halo_nw[turn], 0.0)
        own_w = west_edge[...]
        own_s = south_edge[...]
        corner_b = pltpu.roll(corner_nw, 128 - lane_step, 1)
        col_p, col_s = west_stress(
            west,
            pltpu.roll(west, 128 - lane_step, 1),
            pltpu.roll(west, 128 - 2 * lane_step, 1),
            corner_nw[0:1, :],
            corner_b[0:1, :],
            own_w,
            pltpu.roll(own_w, 128 - lane_step, 1),
            my_col,
        )
        south_a, south_b, south_v = south[0:8], south[8:16], south[16:24]
        row_q, row_s = south_stress(
            south_a,
            south_b,
            south_v,
            lane_column(corner_se[0:8], 0, south_a),
            lane_column(corner_se[8:16], 0, south_b),
            own_s[0:8],
            own_s[8:16],
            mx_row,
        )

        below_v = jnp.where(gz > 0, visc_d[...], 0.0)
        low_a = 4.0 * below_v * (field[0, 0] - jnp.where(gz > 0, halo_d[turn, 0], 0.0))
        low_b = 4.0 * below_v * (field[1, 0] - jnp.where(gz > 0, halo_d[turn, 1], 0.0))
        for k in range(layers):
            va, vb, v = field[0, k], field[1, k], visc[k]
            if k < layers - 1:
                top_a = 4.0 * v * (field[0, k + 1] - va)
                top_b = 4.0 * v * (field[1, k + 1] - vb)
            else:
                top_a = 4.0 * v * (jnp.where(gz < nz - 1, halo_u[turn, 0], 0.0) - va) * up_on
                top_b = 4.0 * v * (jnp.where(gz < nz - 1, halo_u[turn, 1], 0.0) - vb) * up_on
            image_a, image_b = plane_image(
                va,
                vb,
                v,
                lane_column(east, k, va),
                lane_column(east, lane_step + k, vb),
                north[k : k + 1],
                north[row_step + k : row_step + k + 1],
                lane_column(col_p, k, va),
                lane_column(col_s, k, va),
                row_q[k : k + 1],
                row_s[k : k + 1],
                mx,
                my,
            )
            image_a = image_a + (low_a - top_a)
            image_b = image_b + (low_b - top_b)
            if k == 0:
                basal = jnp.where(gz == 0, fric[...], 0.0)
                image_a = image_a + basal * va
                image_b = image_b + basal * vb
            low_a, low_b = top_a, top_b
            damp = damping_of(k)
            store(k, va - damp * image_a, vb - damp * image_b)

    def store_first(k, new_a, new_b):
        middle[0, k] = new_a
        middle[1, k] = new_b

    def store_second(k, new_a, new_b):
        adj_out[0, k] = new_a
        adj_out[1, k] = new_b
        term = slope[0] * new_a + slope[1] * new_b
        if k == 0:
            on_base = jnp.where(gz == 0, 1.0, 0.0)
            land = mask[...].astype(jnp.float32)
            part[0] = -on_base * land * fric[...] * (base[0] * new_a + base[1] * new_b)
            part[1] = term
        elif k < layers - 1:
            part[1] = part[1] + term
        else:
            part[1] = 0.25 * mask[...].astype(jnp.float32) * (part[1] + term)

    def tile_copy(t):
        device = (t // ny, t % ny, gz)
        return remote(
            total.at[0, t], tile_in.at[tile], tile_sem.at[0, t], tile_sem.at[1, tile], device
        )

    def finish(bit, g):
        keep, give, length, _ = starts[bit]
        source = sums if bit == 0 else accs[bit - 1]
        own = pl.ds(*spans[g])
        half_copy(bit, g).wait_recv()
        if bit + 1 < bits:
            next_keep, next_give, next_length, _ = starts[bit + 1]
            for begin in (next_give, next_keep):
                accs[bit][pl.ds(begin, next_length), own] = (
                    source[pl.ds(keep + begin, next_length), own]
                    + recvs[bit][pl.ds(begin, next_length), own]
                )
                if begin is next_give:
                    half_copy(bit + 1, g).start()
            return
        accs[bit][:, own] = source[pl.ds(keep, length), own] + recvs[bit][:, own]
        for t in range(spans[g][0], sum(spans[g])):

            @pl.when(tile != t)
            def _(t=t):
                tile_copy(t).start()

            @pl.when(tile == t)
            def _(t=t):
                tile_in[t] = total[0, t]

    total = accs[bits - 1]

    def part_copy(o):
        device = layer_peers[o - 1]
        begin = pl.multiple_of(device[2] * size, size)
        return remote(
            part.at[:, pl.ds(begin, size), :],
            part_in.at[o - 1],
            part_sem.at[0, o - 1],
            part_sem.at[1, o - 1],
            device,
        )

    prepare()
    bin_group(0)
    pl.semaphore_wait(barrier, nz - 1 + tiles - 1)
    half_copy(0, 0).start()
    visc_up = (
        remote(visc.at[layers - 1], visc_d, visc_sem.at[0], visc_sem.at[1], (gx, gy, gz + 1)),
        gz < nz - 1,
        gz > 0,
    )
    pack(guess)
    first = halo_copies(guess, 0) + [visc_up]
    second = halo_copies(middle, 1)
    start_all(first)

    def early(turn):
        if turn == early_turns[0]:
            wait_receives(first)
            wait_sends(first)
            sweep(guess, 0, store_first)
            pack(middle)
            start_all(second)
        elif turn == early_turns[1]:
            wait_receives(second)
            sweep(middle, 1, store_second)
            for o in range(1, nz):
                part_copy(o).start()
            wait_sends(second)

    turns = groups + 1 + LAG * (bits - 1)
    early_turns = [min(turn, turns - 2 + order) for order, turn in enumerate(EARLY)]
    for turn in range(1, turns):
        if turn < groups:
            bin_group(turn)
            half_copy(0, turn).start()
        for bit in range(bits):
            g = turn - 1 - LAG * bit
            if 0 <= g < groups:
                finish(bit, g)
        early(turn)
    for t in range(tiles):

        @pl.when(tile != t)
        def _(t=t):
            remote(
                total.at[0, t], tile_in.at[t], tile_sem.at[0, t], tile_sem.at[1, t], (t // ny, t % ny, gz)
            ).wait_recv()

    own_rows = pl.ds(pl.multiple_of(gz * size, size), size)
    value = tile_in[0]
    for t in range(1, tiles):
        value = value + tile_in[t]
    land = mask[own_rows, :].astype(jnp.float32)
    value = value * land[None]
    block[...] = value

    lanes = lax.broadcasted_iota(jnp.int32, (size, 128), 1)
    west = jnp.zeros((size, 128), jnp.float32)
    east = jnp.zeros((size, 128), jnp.float32)
    for c in range(2):
        west = jnp.where(lanes == c * lane_step, lane_column(value[c], 0, west), west)
        east = jnp.where(lanes == c * lane_step, lane_column(value[c], cols - 1, east), east)
        edge_s[c * row_step : c * row_step + 1, :] = value[c, 0:1, :]
        edge_n[c * row_step : c * row_step + 1, :] = value[c, size - 1 : size, :]
    edge_w[...] = west
    edge_e[...] = east

    is_top = gz == top
    low = gz == 0

    def ring_one(index, src, dst, slot, device):
        return remote(src, dst, ring_send.at[index], ring_recv.at[slot], device)

    def ring_column(index, src, ring, q, device, slot):
        return ring_one(index, src, ring.at[q], slot, device)

    ring_sends = [
        (ring_one(0, edge_w, ring_e.at[gz], gz, (gx - 1, gy, top)), gx > 0),
        (ring_one(1, edge_e, ring_w.at[gz], nz + gz, (gx + 1, gy, top)), gx < nx - 1),
        (ring_one(2, edge_s, ring_n, 2 * nz, (gx, gy - 1, top)), low & (gy > 0)),
        (ring_one(3, edge_n, ring_s, 2 * nz + 1, (gx, gy + 1, top)), is_top & (gy < ny - 1)),
        (
            ring_one(4, edge_n.at[:, 0:128], ring_se, 2 * nz + 2, (gx - 1, gy + 1, top)),
            is_top & (gx > 0) & (gy < ny - 1),
        ),
        (
            ring_one(5, edge_e.at[0:8, :], ring_nw, 2 * nz + 3, (gx + 1, gy - 1, top)),
            low & (gx < nx - 1) & (gy > 0),
        ),
    ]
    for copy, sends in ring_sends:

        @pl.when(sends)
        def _(copy=copy):
            copy.start()

    to_last = remote(block, forcing.at[gz], last_send, last_recv.at[gz], (gx, gy, top))

    @pl.when(gz < top)
    def _():
        to_last.start()

    def late_copy(j):
        return remote(late.at[j], late_in, late_sem.at[0, j], late_sem.at[1, 0], (gx, gy, j))

    @pl.when(is_top)
    def _():
        forcing[top] = block[...]
        for j in range(top):
            remote(block, forcing.at[j], last_send, last_recv.at[j], (gx, gy, 0)).wait_recv()
        peer = (lax.rem(gx + 1, nx), gy, top)
        for j in range(nz):

            @pl.when(gx < nx - 1)
            def _(j=j):
                ring_one(0, edge_w, ring_e.at[j], j, peer).wait_recv()

            @pl.when(gx > 0)
            def _(j=j):
                ring_one(1, edge_e, ring_w.at[j], nz + j, peer).wait_recv()

        @pl.when(gy < ny - 1)
        def _():
            ring_one(2, edge_s, ring_n, 2 * nz, peer).wait_recv()

        @pl.when(gy > 0)
        def _():
            ring_one(3, edge_n, ring_s, 2 * nz + 1, peer).wait_recv()

        @pl.when((gx < nx - 1) & (gy > 0))
        def _():
            ring_one(4, edge_n.at[:, 0:128], ring_se, 2 * nz + 2, peer).wait_recv()

        @pl.when((gx > 0) & (gy < ny - 1))
        def _():
            ring_one(5, edge_e.at[0:8, :], ring_nw, 2 * nz + 3, peer).wait_recv()

        mx, my = masks()
        my_col = my[:, 0:128]
        mx_row = mx[0:8, :]
        last = layers - 1
        shift = 128 - 2 * lane_step - last

        def scaled(on, force, v):
            return jnp.where(on, force * (0.6 / (18.0 * v)), 0.0)

        def columns(value):
            a = lane_column(value, 0, value)
            return a, lane_column(value, lane_step, value)

        v = visc[last]
        damp = damping_of(last)
        force_a = jnp.concatenate([forcing[q, 0] for q in range(nz)], axis=0)
        force_b = jnp.concatenate([forcing[q, 1] for q in range(nz)], axis=0)
        ea = damp * force_a
        eb = damp * force_b

        west_v = lane_column(halo_w[0], 2 * lane_step + last, halo_w[0])
        east_v = lane_column(halo_e[0], 2 * lane_step + last, halo_e[0])
        south_v = jnp.broadcast_to(halo_s[0, 16 + last : 17 + last, :], (8, cols))
        north_v = jnp.broadcast_to(halo_n[0, 16 + last : 17 + last, :], (8, cols))
        nw_v = lane_column(halo_nw[0], 2 * lane_step + last, halo_nw[0])
        se_v = jnp.broadcast_to(halo_se[0, 16 + last : 17 + last, :], (8, 128))

        ring_w_all = jnp.concatenate([ring_w[q] for q in range(nz)], axis=0)
        ring_e_all = jnp.concatenate([ring_e[q] for q in range(nz)], axis=0)
        west_a, west_b = [scaled(gx > 0, f, west_v) for f in columns(ring_w_all)]
        east_a, east_b = [scaled(gx < nx - 1, f, east_v) for f in columns(ring_e_all)]
        nw_on = (gx > 0) & (gy < ny - 1)
        se_on = (gx < nx - 1) & (gy > 0)
        nw_a, nw_b = [scaled(nw_on, f, nw_v) for f in columns(ring_nw[...])]
        south_a = scaled(gy > 0, ring_s[0:8], south_v)
        south_b = scaled(gy > 0, ring_s[8:16], south_v)
        north_a = scaled(gy < ny - 1, ring_n[0:8], north_v)
        north_b = scaled(gy < ny - 1, ring_n[8:16], north_v)
        se_a = scaled(se_on, ring_se[0:8], se_v)
        se_b = scaled(se_on, ring_se[8:16], se_v)
        west_v = jnp.where(gx > 0, west_v, 0.0)
        south_v = jnp.where(gy > 0, south_v, 0.0)

        col_p, col_s = west_stress(
            west_a,
            west_b,
            west_v,
            nw_a[0:1, :],
            nw_b[0:1, :],
            lane_column(ea, 0, west_a),
            lane_column(eb, 0, west_b),
            my_col,
        )
        row_q, row_s = south_stress(
            south_a,
            south_b,
            south_v,
            lane_column(se_a, 0, south_a),
            lane_column(se_b, 0, south_b),
            jnp.broadcast_to(ea[0:1, :], south_a.shape),
            jnp.broadcast_to(eb[0:1, :], south_b.shape),
            mx_row,
        )
        image_a, image_b = plane_image(
            ea,
            eb,
            v,
            lane_column(east_a, 0, ea),
            lane_column(east_b, 0, eb),
            north_a[0:1],
            north_b[0:1],
            lane_column(col_p, 0, ea),
            lane_column(col_s, 0, ea),
            row_q[0:1],
            row_s[0:1],
            mx,
            my,
        )
        below = 4.0 * visc[last - 1]
        image_a = image_a + below * ea
        image_b = image_b + below * eb
        top_a = ea + damp * (force_a - image_a)
        top_b = eb + damp * (force_b - image_b)
        lift = damping_of(last - 1) * below
        low_a = lift * ea
        low_b = lift * eb
        land = mask[...].astype(jnp.float32)
        drive = 0.25 * land * (slope[0] * (top_a + low_a) + slope[1] * (top_b + low_b))
        for j in range(nz):
            late[j] = drive[j * size : (j + 1) * size, :]
        for j in range(top):
            late_copy(j).start()
        adj_out[0, last] = adj_out[0, last] + top_a
        adj_out[1, last] = adj_out[1, last] + top_b
        adj_out[0, last - 1] = adj_out[0, last - 1] + low_a
        adj_out[1, last - 1] = adj_out[1, last - 1] + low_b
        for j in range(top):
            late_copy(j).wait_send()

    gathered = part[:, own_rows, :]
    for o in range(1, nz):
        part_copy(o).wait_recv()
        gathered = gathered + part_in[o - 1]
    maps_out[0] = gathered[0]

    @pl.when(is_top)
    def _():
        maps_out[1] = gathered[1] + late[top]

    @pl.when(gz < top)
    def _():
        remote(late.at[0], late_in, late_sem.at[0, 0], late_sem.at[1, 0], (gx, gy, top)).wait_recv()
        maps_out[1] = gathered[1] + late_in[...]

    for bit in range(bits):
        for g in range(groups):
            half_copy(bit, g).wait_send()
    for t in range(tiles):

        @pl.when(tile != t)
        def _(t=t):
            tile_copy(t).wait_send()

    @pl.when(gz < top)
    def _():
        to_last.wait_send()

    for copy, sends in ring_sends:

        @pl.when(sends)
        def _(copy=copy):
            copy.wait_send()

    for o in range(1, nz):
        part_copy(o).wait_send()


def apply_twice(count, pixels, guess, visc, fric, base, slope, mask, counts):
    nx, ny, nz = counts
    tiles = nx * ny
    bits = nz.bit_length() - 1
    _, layers, rows, cols = guess.shape
    size = rows // nz
    f32 = jnp.float32
    groups = len(tile_spans(tiles))
    per_device = pixels[0].shape[0]
    cap = 2 * per_device // tiles
    chunk_rows = min(8, cap // 128)
    depth = chunk_rows * 128
    chunks = cap // depth
    flat = [value.reshape(per_device // 128, 128) for value in pixels]
    halves = [pltpu.VMEM((nz >> (bit + 1), tiles, 2, size, cols), f32) for bit in range(bits)]
    vmem = pl.BlockSpec(memory_space=pltpu.VMEM)
    dma = pltpu.SemaphoreType.DMA
    return pl.pallas_call(
        functools.partial(apply_kernel, counts),
        in_specs=[pl.BlockSpec(memory_space=pltpu.SMEM)] + [vmem] * 10,
        out_specs=(vmem, vmem),
        out_shape=(pltpu.VMEM(guess.shape, f32), pltpu.VMEM((2, size, cols), f32)),
        scratch_shapes=halves
        + halves
        + [
            pltpu.VMEM((6, tiles * chunks, chunk_rows, 128), f32),
            pltpu.VMEM((nz, tiles, 2, size, cols), f32),
            pltpu.VMEM((chunks, 4 * rows, depth), jnp.bfloat16),
            pltpu.VMEM((chunks, cols, depth), jnp.bfloat16),
            pltpu.VMEM((4 * rows, cols), f32),
            pltpu.VMEM((tiles, 2, size, cols), f32),
            pltpu.VMEM((2, size, cols), f32),
            pltpu.VMEM((nz, 2, size, cols), f32),
            pltpu.VMEM(guess.shape, f32),
            pltpu.VMEM((rows, 128), f32),
            pltpu.VMEM((rows, 128), f32),
            pltpu.VMEM((24, cols), f32),
            pltpu.VMEM((24, cols), f32),
            pltpu.VMEM((2, rows, 128), f32),
            pltpu.VMEM((2, rows, 128), f32),
            pltpu.VMEM((2, 24, cols), f32),
            pltpu.VMEM((2, 24, cols), f32),
            pltpu.VMEM((2, 24, 128), f32),
            pltpu.VMEM((2, 8, 128), f32),
            pltpu.VMEM((2, 2, rows, cols), f32),
            pltpu.VMEM((2, 2, rows, cols), f32),
            pltpu.VMEM((rows, cols), f32),
            pltpu.VMEM((2, rows, cols), f32),
            pltpu.VMEM((nz - 1, 2, size, cols), f32),
            pltpu.VMEM((size, 128), f32),
            pltpu.VMEM((size, 128), f32),
            pltpu.VMEM((16, cols), f32),
            pltpu.VMEM((16, cols), f32),
            pltpu.VMEM((nz, size, 128), f32),
            pltpu.VMEM((nz, size, 128), f32),
            pltpu.VMEM((16, cols), f32),
            pltpu.VMEM((16, cols), f32),
            pltpu.VMEM((16, 128), f32),
            pltpu.VMEM((8, 128), f32),
            pltpu.VMEM((nz, size, cols), f32),
            pltpu.VMEM((size, cols), f32),
            dma((2, bits, groups)),
            dma((2, tiles)),
            dma,
            dma((nz,)),
            dma((2, 2, 8)),
            dma((2,)),
            dma((2, nz - 1)),
            dma((6,)),
            dma((2 * nz + 4,)),
            dma((2, nz)),
        ],
        compiler_params=pltpu.CompilerParams(
            collective_id=0, has_side_effects=True, vmem_limit_bytes=56 * 2**20
        ),
        name="apply_twice",
    )(count, *flat, guess, visc, fric, base, slope, mask)


def body(
    adjoint_guess,
    viscosity,
    friction,
    base_velocity,
    surface_slope,
    ice_mask,
    pixel_misfit,
    pixel_look,
    pixel_tile,
    pixel_cell,
    pixel_count,
):
    sizes = tuple(lax.axis_size(name) for name in ("gx", "gy", "gz"))
    pixels = (pixel_misfit, pixel_look, pixel_tile[:, 0], pixel_cell)
    return apply_twice(
        pixel_count,
        pixels,
        adjoint_guess,
        viscosity,
        friction,
        base_velocity,
        surface_slope,
        ice_mask,
        sizes,
    )


def solution(mesh):
    return jax.shard_map(
        body,
        mesh=mesh,
        in_specs=(
            P(None, "gz", "gy", "gx"),
            P("gz", "gy", "gx"),
            P("gy", "gx"),
            P(None, "gy", "gx"),
            P(None, "gy", "gx"),
            P("gy", "gx"),
            P(("gx", "gy", "gz")),
            P(("gx", "gy", "gz")),
            P(("gx", "gy", "gz"), None),
            P(("gx", "gy", "gz")),
            P(("gx", "gy", "gz")),
        ),
        out_specs=(P(None, "gz", "gy", "gx"), P(None, ("gy", "gz"), "gx")),
        check_vma=False,
    )
```

```python
import functools
import math

import jax
import jax.numpy as jnp
from jax import lax
from jax.experimental import pallas as pl
from jax.experimental.pallas import tpu as pltpu
from jax.sharding import PartitionSpec as P

SHARES = (2, 2, 2, 2)
EARLY = (3, 5)
LAG = 2


def lane_column(pack, lane, like):
    return jnp.broadcast_to(pack[:, lane : lane + 1], like.shape)


def from_east(value, column):
    size = value.shape[1]
    lanes = lax.broadcasted_iota(jnp.int32, value.shape, 1)
    return jnp.where(lanes == size - 1, column, pltpu.roll(value, size - 1, 1))


def from_west(value, column):
    lanes = lax.broadcasted_iota(jnp.int32, value.shape, 1)
    return jnp.where(lanes == 0, column, pltpu.roll(value, 1, 1))


def from_north(value, row):
    size = value.shape[0]
    rows = lax.broadcasted_iota(jnp.int32, value.shape, 0)
    return jnp.where(rows == size - 1, row, pltpu.roll(value, size - 1, 0))


def from_south(value, row):
    rows = lax.broadcasted_iota(jnp.int32, value.shape, 0)
    return jnp.where(rows == 0, row, pltpu.roll(value, 1, 0))


def reverse_bits(value, bits):
    out = 0
    for bit in range(bits):
        out |= ((value >> bit) & 1) << (bits - 1 - bit)
    return out


def sin_cos(angle):
    turns = jnp.floor(angle * (2.0 / math.pi) + 0.5)
    rest = angle - turns * 1.5703125
    rest = rest - turns * 4.837512969970703125e-4
    rest = rest - turns * 7.54978995489188e-8
    square = rest * rest
    sine = -1.9515295891e-4 * square + 8.3321608736e-3
    sine = (sine * square - 1.6666654611e-1) * square * rest + rest
    cosine = 2.443315711809948e-5 * square - 1.388731625493765e-3
    cosine = (cosine * square + 4.166664568298827e-2) * square * square
    cosine = cosine - 0.5 * square + 1.0
    quadrant = turns.astype(jnp.int32) & 3
    swap = (quadrant & 1) == 1
    first = jnp.where(swap, cosine, sine)
    second = jnp.where(swap, sine, cosine)
    out_sine = jnp.where(quadrant >= 2, -first, first)
    out_cosine = jnp.where((quadrant == 1) | (quadrant == 2), -second, second)
    return out_sine, out_cosine


def exchange(words, bit, inner):
    blocks, sublanes, lanes = words[0].shape
    vregs = inner.bit_length() - 1
    if bit < vregs or bit >= vregs + 10:
        half = 1 << bit if bit < vregs else inner
        shape = (blocks // (2 * half), 2, half, sublanes, lanes)
        parts = [word.reshape(shape) for word in words]
        lower = [part[:, 0] for part in parts]
        upper = [part[:, 1] for part in parts]
        swap = lower[0] > upper[0]
        out = []
        for a, b in zip(lower, upper):
            first = jnp.where(swap, b, a)
            second = jnp.where(swap, a, b)
            out.append(jnp.stack([first, second], axis=1).reshape(blocks, sublanes, lanes))
        return out
    axis = 1 if bit < vregs + 3 else 2
    step = 1 << (bit - vregs) if axis == 1 else 1 << (bit - vregs - 3)
    size = (sublanes, lanes)[axis - 1]
    spots = lax.broadcasted_iota(jnp.int32, (1, sublanes, lanes), axis)
    high = jnp.broadcast_to((spots & step) != 0, words[0].shape)
    sign = jnp.where((spots & step) != 0, -1.0, 1.0)
    partners = []
    for word in words:
        back = pltpu.roll(word, step, axis)
        if 2 * step == size:
            partners.append(back)
        else:
            partners.append(jnp.where(high, back, pltpu.roll(word, size - step, axis)))
    take = (partners[0] - words[0]) * sign < 0.0
    return [jnp.where(take, partner, word) for partner, word in zip(partners, words)]


def order_bit(shape, bit):
    vregs = shape[0].bit_length() - 1
    if bit < vregs:
        return lax.broadcasted_iota(jnp.int32, shape, 0) & (1 << bit)
    if bit < vregs + 3:
        return lax.broadcasted_iota(jnp.int32, shape, 1) & (1 << (bit - vregs))
    return lax.broadcasted_iota(jnp.int32, shape, 2) & (1 << (bit - vregs - 3))


def order_of(shape):
    block = lax.broadcasted_iota(jnp.int32, shape, 0)
    row = lax.broadcasted_iota(jnp.int32, shape, 1)
    lane = lax.broadcasted_iota(jnp.int32, shape, 2)
    return (lane * shape[1] + row) * shape[0] + block


def sort_words(words):
    shape = words[0].shape
    bits = math.prod(shape).bit_length() - 1
    key, rest = words[0], list(words[1:])
    sign = None
    for phase in range(1, bits + 1):
        after = 1.0
        if phase < bits:
            after = jnp.where(order_bit(shape, phase) != 0, -1.0, 1.0)
        turn = after if sign is None else after * sign
        key = key * turn
        sign = after
        for bit in reversed(range(phase)):
            key, *rest = exchange([key] + rest, bit, shape[0])
    return [key] + rest


def tile_spans(tiles):
    if tiles % sum(SHARES):
        return [(0, tiles)]
    unit = tiles // sum(SHARES)
    return [(sum(SHARES[:g]) * unit, share * unit) for g, share in enumerate(SHARES)]


def apply_kernel(
    counts,
    count_ref,
    misfit_ref,
    look_ref,
    tile_ref,
    cell_ref,
    guess,
    visc,
    fric,
    base,
    slope,
    mask,
    adj_out,
    maps_out,
    *scratch,
):
    nx, ny, nz = counts
    bits = nz.bit_length() - 1
    tiles = nx * ny
    layers, rows, cols = visc.shape
    size = rows // nz
    spans = tile_spans(tiles)
    groups = len(spans)
    scratch = list(scratch)
    accs = [scratch.pop(0) for _ in range(bits)]
    recvs = [scratch.pop(0) for _ in range(bits)]
    (
        pixels,
        sums,
        lhs,
        rhs,
        acc,
        tile_in,
        block,
        forcing,
        middle,
        west_edge,
        east_edge,
        south_edge,
        north_edge,
        halo_w,
        halo_e,
        halo_s,
        halo_n,
        halo_se,
        halo_nw,
        halo_d,
        halo_u,
        visc_d,
        part,
        part_in,
        edge_w,
        edge_e,
        edge_s,
        edge_n,
        ring_w,
        ring_e,
        ring_s,
        ring_n,
        ring_se,
        ring_nw,
        late,
        late_in,
        half_sem,
        tile_sem,
        last_send,
        last_recv,
        halo_sem,
        visc_sem,
        part_sem,
        ring_send,
        ring_recv,
        late_sem,
    ) = scratch
    chunks, chunk_rows = pixels.shape[1] // tiles, pixels.shape[2]
    gx, gy, gz = lax.axis_index("gx"), lax.axis_index("gy"), lax.axis_index("gz")
    tile = gx * ny + gy
    lane_step = 16
    row_step = 8
    top = nz - 1

    def remote(src, dst, send, recv, device):
        return pltpu.make_async_remote_copy(
            src_ref=src,
            dst_ref=dst,
            send_sem=send,
            recv_sem=recv,
            device_id=device,
            device_id_type=pl.DeviceIdType.MESH,
        )

    barrier = pltpu.get_barrier_semaphore()
    layer_peers = [(gx, gy, lax.rem(gz + o, nz)) for o in range(1, nz)]
    tile_peers = []
    for o in range(1, tiles):
        other = lax.rem(tile + o, tiles)
        tile_peers.append((other, (lax.div(other, ny), lax.rem(other, ny), gz)))
    for device in layer_peers + [device for _, device in tile_peers]:
        pl.semaphore_signal(barrier, inc=1, device_id=device, device_id_type=pl.DeviceIdType.MESH)

    def prepare():
        sine, cosine = sin_cos(look_ref[...])
        order = lax.broadcasted_iota(jnp.int32, misfit_ref.shape, 0) * misfit_ref.shape[1]
        order = order + lax.broadcasted_iota(jnp.int32, misfit_ref.shape, 1)
        value = jnp.where(order < count_ref[0], misfit_ref[...], 0.0)
        total_rows, lanes = misfit_ref.shape
        cells = rows * cols
        cap = chunks * chunk_rows * lanes
        names = tile_ref[...]
        key = (names * cells + cell_ref[...]).astype(jnp.float32)
        shape = (total_rows // 8, 8, lanes)
        words = [word.reshape(shape) for word in (key, value * cosine, value * sine)]
        words = sort_words(words)
        place = total_rows * lanes - 1 - order_of(shape)
        filler = jnp.zeros(shape, jnp.float32)
        for t in range(tiles - 1):
            below = jnp.where(names <= t, 1.0, 0.0)
            below = jnp.sum(jnp.sum(below, axis=0, keepdims=True), axis=1, keepdims=True)
            spare = (float(cap * (t + 1)) - below).reshape(1, 1, 1)
            filler = filler + jnp.where(place.astype(jnp.float32) >= spare, float(cells), 0.0)
        zero = jnp.zeros(shape, jnp.float32)
        words = [jnp.concatenate(pair, axis=0) for pair in zip(words, (filler, zero, zero))]
        for bit in reversed(range((total_rows * lanes).bit_length())):
            words = exchange(words, bit, shape[0])
        width = chunk_rows
        for side in range(2):
            half = slice(side * shape[0], (side + 1) * shape[0])
            key, fx, fy = [word[half].reshape(total_rows, lanes).T for word in words]
            spots = lax.broadcasted_iota(jnp.int32, (lanes, total_rows), 0) + side * lanes
            owner = lax.div(spots * total_rows, cap).astype(jnp.float32)
            cell = key - owner * float(cells)
            row = jnp.floor((cell + 0.5) * (1.0 / cols))
            fields = []
            for f in (fx, fy):
                high = f.astype(jnp.bfloat16).astype(jnp.float32)
                fields += [high, f - high]
            fields += [row, cell - row * float(cols)]
            for f, field in enumerate(fields):
                for r in range(lanes // width):
                    pixels[f, side * (lanes // width) + r] = field[r * width : (r + 1) * width, :]

    starts = []
    length = nz // 2
    for bit in range(bits):
        own_bit = lax.rem(lax.div(gz, 1 << bit), 2)
        keep = own_bit * length
        give = (1 - own_bit) * length
        peer = (gx, gy, gz + (1 - 2 * own_bit) * (1 << bit))
        starts.append((keep, give, length, peer))
        length //= 2

    def half_copy(bit, g):
        _, give, length, peer = starts[bit]
        source = sums if bit == 0 else accs[bit - 1]
        own = pl.ds(*spans[g])
        return remote(
            source.at[pl.ds(give, length), own],
            recvs[bit].at[:, own],
            half_sem.at[0, bit, g],
            half_sem.at[1, bit, g],
            peer,
        )

    def bin_group(g):
        def build(i, slot):
            ids = lax.broadcasted_iota(jnp.int32, (cols, 128), 0)
            ids = ids.astype(jnp.float32).astype(jnp.bfloat16)
            row_ids = lax.broadcasted_iota(jnp.int32, (rows, 128), 0)
            row_ids = row_ids.astype(jnp.float32).astype(jnp.bfloat16)
            one = jnp.ones((cols, 128), jnp.bfloat16)
            none = jnp.zeros((cols, 128), jnp.bfloat16)
            zero = jnp.zeros((rows, 128), jnp.bfloat16)
            fields = [pixels[f, i] for f in range(6)]

            def spread(field, j, length):
                strip = jnp.broadcast_to(field[j : j + 1, :], (16, 128)).astype(jnp.bfloat16)
                return jnp.concatenate([strip] * (length // 16), axis=0)

            for j in range(chunk_rows):
                span = slice(j * 128, (j + 1) * 128)
                rhs[slot, :, span] = jnp.where(ids == spread(fields[5], j, cols), one, none)
                hit = row_ids == spread(fields[4], j, rows)
                for f in range(4):
                    start = ((f % 2) * 2 + f // 2) * rows
                    piece = spread(fields[f], j, rows)
                    lhs[slot, start : start + rows, span] = jnp.where(hit, piece, zero)

        def one_tile(n, carry):
            t = spans[g][0] + n
            for slot in range(chunks):
                build(t * chunks + slot, slot)
                product = lax.dot_general(
                    lhs[slot], rhs[slot], (((1,), (1,)), ((), ())), preferred_element_type=jnp.float32
                )
                if slot == 0:
                    acc[...] = product
                else:
                    acc[...] += product
            half = 2 * rows
            for c in range(2):
                for q in range(nz):
                    begin = c * rows + q * size
                    sums[reverse_bits(q, bits), t, c] = (
                        acc[begin : begin + size] + acc[half + begin : half + begin + size]
                    )
            return carry

        lax.fori_loop(0, spans[g][1], one_tile, 0)

    def pack(field):
        lanes = lax.broadcasted_iota(jnp.int32, (rows, 128), 1)
        west = jnp.zeros((rows, 128), jnp.float32)
        east = jnp.zeros((rows, 128), jnp.float32)
        for f in range(3):
            for k in range(layers):
                value = field[f, k] if f < 2 else visc[k]
                south_edge[f * row_step + k : f * row_step + k + 1, :] = value[0:1, :]
                north_edge[f * row_step + k : f * row_step + k + 1, :] = value[rows - 1 : rows, :]
                lane = lanes == f * lane_step + k
                west = jnp.where(lane, lane_column(value, 0, west), west)
                east = jnp.where(lane, lane_column(value, cols - 1, east), east)
        west_edge[...] = west
        east_edge[...] = east

    def halo_copies(field, turn):
        def one(index, src, dst, device):
            return remote(src, dst, halo_sem.at[turn, 0, index], halo_sem.at[turn, 1, index], device)

        return [
            (one(0, west_edge, halo_e.at[turn], (gx - 1, gy, gz)), gx > 0, gx < nx - 1),
            (one(1, east_edge, halo_w.at[turn], (gx + 1, gy, gz)), gx < nx - 1, gx > 0),
            (one(2, south_edge, halo_n.at[turn], (gx, gy - 1, gz)), gy > 0, gy < ny - 1),
            (one(3, north_edge, halo_s.at[turn], (gx, gy + 1, gz)), gy < ny - 1, gy > 0),
            (
                one(4, north_edge.at[:, 0:128], halo_se.at[turn], (gx - 1, gy + 1, gz)),
                (gx > 0) & (gy < ny - 1),
                (gx < nx - 1) & (gy > 0),
            ),
            (
                one(5, east_edge.at[0:8, :], halo_nw.at[turn], (gx + 1, gy - 1, gz)),
                (gx < nx - 1) & (gy > 0),
                (gx > 0) & (gy < ny - 1),
            ),
            (one(6, field.at[:, 0], halo_u.at[turn], (gx, gy, gz - 1)), gz > 0, gz < nz - 1),
            (one(7, field.at[:, layers - 1], halo_d.at[turn], (gx, gy, gz + 1)), gz < nz - 1, gz > 0),
        ]

    def start_all(copies):
        for copy, sends, _ in copies:

            @pl.when(sends)
            def _(copy=copy):
                copy.start()

    def wait_receives(copies):
        for copy, _, receives in copies:

            @pl.when(receives)
            def _(copy=copy):
                copy.wait_recv()

    def wait_sends(copies):
        for copy, sends, _ in copies:

            @pl.when(sends)
            def _(copy=copy):
                copy.wait_send()

    lane_ids = lax.broadcasted_iota(jnp.int32, (rows, cols), 1)
    row_ids = lax.broadcasted_iota(jnp.int32, (rows, cols), 0)

    def masks():
        mx = jnp.where((lane_ids < cols - 1) | (gx < nx - 1), 1.0, 0.0)
        my = jnp.where((row_ids < rows - 1) | (gy < ny - 1), 1.0, 0.0)
        return mx, my

    west_on = jnp.where(gx > 0, 1.0, 0.0)
    south_on = jnp.where(gy > 0, 1.0, 0.0)
    up_on = jnp.where(gz < nz - 1, 1.0, 0.0)

    def damping_of(k):
        scale = 18.0 * visc[k]
        if k == 0:
            scale = scale + jnp.where(gz == 0, fric[...], 0.0)
        return 0.6 / scale

    def west_stress(a, b, v, corner_a, corner_b, own_a, own_b, my_col):
        na = (from_north(a, corner_a) - a) * my_col
        nb = (from_north(b, corner_b) - b) * my_col
        ea = (own_a - a) * west_on
        eb = (own_b - b) * west_on
        return v * (4.0 * ea + 2.0 * nb) * west_on, v * (na + eb) * west_on

    def south_stress(a, b, v, corner_a, corner_b, own_a, own_b, mx_row):
        ea = (from_east(a, corner_a) - a) * mx_row
        eb = (from_east(b, corner_b) - b) * mx_row
        na = (own_a - a) * south_on
        nb = (own_b - b) * south_on
        return v * (4.0 * nb + 2.0 * ea) * south_on, v * (na + eb) * south_on

    def plane_image(va, vb, v, east_a, east_b, north_a, north_b, col_p, col_s, row_q, row_s, mx, my):
        ea = (from_east(va, east_a) - va) * mx
        eb = (from_east(vb, east_b) - vb) * mx
        na = (from_north(va, north_a) - va) * my
        nb = (from_north(vb, north_b) - vb) * my
        p = mx * v * (4.0 * ea + 2.0 * nb)
        q = my * v * (4.0 * nb + 2.0 * ea)
        s = v * (na + eb)
        sx = mx * s
        sy = my * s
        image_a = (from_west(p, col_p) - p) + (from_south(sy, row_s) - sy)
        image_b = (from_south(q, row_q) - q) + (from_west(sx, col_s) - sx)
        return image_a, image_b

    def sweep(field, turn, store):
        mx, my = masks()
        my_col = my[:, 0:128]
        mx_row = mx[0:8, :]
        west = jnp.where(gx > 0, halo_w[turn], 0.0)
        east = jnp.where(gx < nx - 1, halo_e[turn], 0.0)
        south = jnp.where(gy > 0, halo_s[turn], 0.0)
        north = jnp.where(gy < ny - 1, halo_n[turn], 0.0)
        corner_se = jnp.where((gx < nx - 1) & (gy > 0), halo_se[turn], 0.0)
        corner_nw = jnp.where((gx > 0) & (gy < ny - 1), halo_nw[turn], 0.0)
        own_w = west_edge[...]
        own_s = south_edge[...]
        corner_b = pltpu.roll(corner_nw, 128 - lane_step, 1)
        col_p, col_s = west_stress(
            west,
            pltpu.roll(west, 128 - lane_step, 1),
            pltpu.roll(west, 128 - 2 * lane_step, 1),
            corner_nw[0:1, :],
            corner_b[0:1, :],
            own_w,
            pltpu.roll(own_w, 128 - lane_step, 1),
            my_col,
        )
        south_a, south_b, south_v = south[0:8], south[8:16], south[16:24]
        row_q, row_s = south_stress(
            south_a,
            south_b,
            south_v,
            lane_column(corner_se[0:8], 0, south_a),
            lane_column(corner_se[8:16], 0, south_b),
            own_s[0:8],
            own_s[8:16],
            mx_row,
        )

        below_v = jnp.where(gz > 0, visc_d[...], 0.0)
        low_a = 4.0 * below_v * (field[0, 0] - jnp.where(gz > 0, halo_d[turn, 0], 0.0))
        low_b = 4.0 * below_v * (field[1, 0] - jnp.where(gz > 0, halo_d[turn, 1], 0.0))
        for k in range(layers):
            va, vb, v = field[0, k], field[1, k], visc[k]
            if k < layers - 1:
                top_a = 4.0 * v * (field[0, k + 1] - va)
                top_b = 4.0 * v * (field[1, k + 1] - vb)
            else:
                top_a = 4.0 * v * (jnp.where(gz < nz - 1, halo_u[turn, 0], 0.0) - va) * up_on
                top_b = 4.0 * v * (jnp.where(gz < nz - 1, halo_u[turn, 1], 0.0) - vb) * up_on
            image_a, image_b = plane_image(
                va,
                vb,
                v,
                lane_column(east, k, va),
                lane_column(east, lane_step + k, vb),
                north[k : k + 1],
                north[row_step + k : row_step + k + 1],
                lane_column(col_p, k, va),
                lane_column(col_s, k, va),
                row_q[k : k + 1],
                row_s[k : k + 1],
                mx,
                my,
            )
            image_a = image_a + (low_a - top_a)
            image_b = image_b + (low_b - top_b)
            if k == 0:
                basal = jnp.where(gz == 0, fric[...], 0.0)
                image_a = image_a + basal * va
                image_b = image_b + basal * vb
            low_a, low_b = top_a, top_b
            damp = damping_of(k)
            store(k, va - damp * image_a, vb - damp * image_b)

    def store_first(k, new_a, new_b):
        middle[0, k] = new_a
        middle[1, k] = new_b

    def store_second(k, new_a, new_b):
        adj_out[0, k] = new_a
        adj_out[1, k] = new_b
        term = slope[0] * new_a + slope[1] * new_b
        if k == 0:
            on_base = jnp.where(gz == 0, 1.0, 0.0)
            land = mask[...].astype(jnp.float32)
            part[0] = -on_base * land * fric[...] * (base[0] * new_a + base[1] * new_b)
            part[1] = term
        elif k < layers - 1:
            part[1] = part[1] + term
        else:
            part[1] = 0.25 * mask[...].astype(jnp.float32) * (part[1] + term)

    def tile_copy(t):
        device = (t // ny, t % ny, gz)
        return remote(
            total.at[0, t], tile_in.at[tile], tile_sem.at[0, t], tile_sem.at[1, tile], device
        )

    def finish(bit, g):
        keep, give, length, _ = starts[bit]
        source = sums if bit == 0 else accs[bit - 1]
        own = pl.ds(*spans[g])
        half_copy(bit, g).wait_recv()
        if bit + 1 < bits:
            next_keep, next_give, next_length, _ = starts[bit + 1]
            for begin in (next_give, next_keep):
                accs[bit][pl.ds(begin, next_length), own] = (
                    source[pl.ds(keep + begin, next_length), own]
                    + recvs[bit][pl.ds(begin, next_length), own]
                )
                if begin is next_give:
                    half_copy(bit + 1, g).start()
            return
        accs[bit][:, own] = source[pl.ds(keep, length), own] + recvs[bit][:, own]
        for t in range(spans[g][0], sum(spans[g])):

            @pl.when(tile != t)
            def _(t=t):
                tile_copy(t).start()

            @pl.when(tile == t)
            def _(t=t):
                tile_in[t] = total[0, t]

    total = accs[bits - 1]

    def part_copy(o):
        device = layer_peers[o - 1]
        begin = pl.multiple_of(device[2] * size, size)
        return remote(
            part.at[:, pl.ds(begin, size), :],
            part_in.at[o - 1],
            part_sem.at[0, o - 1],
            part_sem.at[1, o - 1],
            device,
        )

    prepare()
    bin_group(0)
    pl.semaphore_wait(barrier, nz - 1 + tiles - 1)
    half_copy(0, 0).start()
    visc_up = (
        remote(visc.at[layers - 1], visc_d, visc_sem.at[0], visc_sem.at[1], (gx, gy, gz + 1)),
        gz < nz - 1,
        gz > 0,
    )
    pack(guess)
    first = halo_copies(guess, 0) + [visc_up]
    second = halo_copies(middle, 1)
    start_all(first)

    def early(turn):
        if turn == early_turns[0]:
            wait_receives(first)
            wait_sends(first)
            sweep(guess, 0, store_first)
            pack(middle)
            start_all(second)
        elif turn == early_turns[1]:
            wait_receives(second)
            sweep(middle, 1, store_second)
            for o in range(1, nz):
                part_copy(o).start()
            wait_sends(second)

    turns = groups + 1 + LAG * (bits - 1)
    early_turns = [min(turn, turns - 2 + order) for order, turn in enumerate(EARLY)]
    for turn in range(1, turns):
        if turn < groups:
            bin_group(turn)
            half_copy(0, turn).start()
        for bit in range(bits):
            g = turn - 1 - LAG * bit
            if 0 <= g < groups:
                finish(bit, g)
        early(turn)
    for t in range(tiles):

        @pl.when(tile != t)
        def _(t=t):
            remote(
                total.at[0, t], tile_in.at[t], tile_sem.at[0, t], tile_sem.at[1, t], (t // ny, t % ny, gz)
            ).wait_recv()

    own_rows = pl.ds(pl.multiple_of(gz * size, size), size)
    value = tile_in[0]
    for t in range(1, tiles):
        value = value + tile_in[t]
    land = mask[own_rows, :].astype(jnp.float32)
    value = value * land[None]
    block[...] = value

    lanes = lax.broadcasted_iota(jnp.int32, (size, 128), 1)
    west = jnp.zeros((size, 128), jnp.float32)
    east = jnp.zeros((size, 128), jnp.float32)
    for c in range(2):
        west = jnp.where(lanes == c * lane_step, lane_column(value[c], 0, west), west)
        east = jnp.where(lanes == c * lane_step, lane_column(value[c], cols - 1, east), east)
        edge_s[c * row_step : c * row_step + 1, :] = value[c, 0:1, :]
        edge_n[c * row_step : c * row_step + 1, :] = value[c, size - 1 : size, :]
    edge_w[...] = west
    edge_e[...] = east

    is_top = gz == top
    low = gz == 0

    def ring_one(index, src, dst, slot, device):
        return remote(src, dst, ring_send.at[index], ring_recv.at[slot], device)

    def ring_column(index, src, ring, q, device, slot):
        return ring_one(index, src, ring.at[q], slot, device)

    ring_sends = [
        (ring_one(0, edge_w, ring_e.at[gz], gz, (gx - 1, gy, top)), gx > 0),
        (ring_one(1, edge_e, ring_w.at[gz], nz + gz, (gx + 1, gy, top)), gx < nx - 1),
        (ring_one(2, edge_s, ring_n, 2 * nz, (gx, gy - 1, top)), low & (gy > 0)),
        (ring_one(3, edge_n, ring_s, 2 * nz + 1, (gx, gy + 1, top)), is_top & (gy < ny - 1)),
        (
            ring_one(4, edge_n.at[:, 0:128], ring_se, 2 * nz + 2, (gx - 1, gy + 1, top)),
            is_top & (gx > 0) & (gy < ny - 1),
        ),
        (
            ring_one(5, edge_e.at[0:8, :], ring_nw, 2 * nz + 3, (gx + 1, gy - 1, top)),
            low & (gx < nx - 1) & (gy > 0),
        ),
    ]
    for copy, sends in ring_sends:

        @pl.when(sends)
        def _(copy=copy):
            copy.start()

    to_last = remote(block, forcing.at[gz], last_send, last_recv.at[gz], (gx, gy, top))

    @pl.when(gz < top)
    def _():
        to_last.start()

    def late_copy(j):
        return remote(late.at[j], late_in, late_sem.at[0, j], late_sem.at[1, 0], (gx, gy, j))

    @pl.when(is_top)
    def _():
        forcing[top] = block[...]
        for j in range(top):
            remote(block, forcing.at[j], last_send, last_recv.at[j], (gx, gy, 0)).wait_recv()
        peer = (lax.rem(gx + 1, nx), gy, top)
        for j in range(nz):

            @pl.when(gx < nx - 1)
            def _(j=j):
                ring_one(0, edge_w, ring_e.at[j], j, peer).wait_recv()

            @pl.when(gx > 0)
            def _(j=j):
                ring_one(1, edge_e, ring_w.at[j], nz + j, peer).wait_recv()

        @pl.when(gy < ny - 1)
        def _():
            ring_one(2, edge_s, ring_n, 2 * nz, peer).wait_recv()

        @pl.when(gy > 0)
        def _():
            ring_one(3, edge_n, ring_s, 2 * nz + 1, peer).wait_recv()

        @pl.when((gx < nx - 1) & (gy > 0))
        def _():
            ring_one(4, edge_n.at[:, 0:128], ring_se, 2 * nz + 2, peer).wait_recv()

        @pl.when((gx > 0) & (gy < ny - 1))
        def _():
            ring_one(5, edge_e.at[0:8, :], ring_nw, 2 * nz + 3, peer).wait_recv()

        mx, my = masks()
        my_col = my[:, 0:128]
        mx_row = mx[0:8, :]
        last = layers - 1
        shift = 128 - 2 * lane_step - last

        def scaled(on, force, v):
            return jnp.where(on, force * (0.6 / (18.0 * v)), 0.0)

        def columns(value):
            a = lane_column(value, 0, value)
            return a, lane_column(value, lane_step, value)

        v = visc[last]
        damp = damping_of(last)
        force_a = jnp.concatenate([forcing[q, 0] for q in range(nz)], axis=0)
        force_b = jnp.concatenate([forcing[q, 1] for q in range(nz)], axis=0)
        ea = damp * force_a
        eb = damp * force_b

        west_v = lane_column(halo_w[0], 2 * lane_step + last, halo_w[0])
        east_v = lane_column(halo_e[0], 2 * lane_step + last, halo_e[0])
        south_v = jnp.broadcast_to(halo_s[0, 16 + last : 17 + last, :], (8, cols))
        north_v = jnp.broadcast_to(halo_n[0, 16 + last : 17 + last, :], (8, cols))
        nw_v = lane_column(halo_nw[0], 2 * lane_step + last, halo_nw[0])
        se_v = jnp.broadcast_to(halo_se[0, 16 + last : 17 + last, :], (8, 128))

        ring_w_all = jnp.concatenate([ring_w[q] for q in range(nz)], axis=0)
        ring_e_all = jnp.concatenate([ring_e[q] for q in range(nz)], axis=0)
        west_a, west_b = [scaled(gx > 0, f, west_v) for f in columns(ring_w_all)]
        east_a, east_b = [scaled(gx < nx - 1, f, east_v) for f in columns(ring_e_all)]
        nw_on = (gx > 0) & (gy < ny - 1)
        se_on = (gx < nx - 1) & (gy > 0)
        nw_a, nw_b = [scaled(nw_on, f, nw_v) for f in columns(ring_nw[...])]
        south_a = scaled(gy > 0, ring_s[0:8], south_v)
        south_b = scaled(gy > 0, ring_s[8:16], south_v)
        north_a = scaled(gy < ny - 1, ring_n[0:8], north_v)
        north_b = scaled(gy < ny - 1, ring_n[8:16], north_v)
        se_a = scaled(se_on, ring_se[0:8], se_v)
        se_b = scaled(se_on, ring_se[8:16], se_v)
        west_v = jnp.where(gx > 0, west_v, 0.0)
        south_v = jnp.where(gy > 0, south_v, 0.0)

        col_p, col_s = west_stress(
            west_a,
            west_b,
            west_v,
            nw_a[0:1, :],
            nw_b[0:1, :],
            lane_column(ea, 0, west_a),
            lane_column(eb, 0, west_b),
            my_col,
        )
        row_q, row_s = south_stress(
            south_a,
            south_b,
            south_v,
            lane_column(se_a, 0, south_a),
            lane_column(se_b, 0, south_b),
            jnp.broadcast_to(ea[0:1, :], south_a.shape),
            jnp.broadcast_to(eb[0:1, :], south_b.shape),
            mx_row,
        )
        image_a, image_b = plane_image(
            ea,
            eb,
            v,
            lane_column(east_a, 0, ea),
            lane_column(east_b, 0, eb),
            north_a[0:1],
            north_b[0:1],
            lane_column(col_p, 0, ea),
            lane_column(col_s, 0, ea),
            row_q[0:1],
            row_s[0:1],
            mx,
            my,
        )
        below = 4.0 * visc[last - 1]
        image_a = image_a + below * ea
        image_b = image_b + below * eb
        top_a = ea + damp * (force_a - image_a)
        top_b = eb + damp * (force_b - image_b)
        lift = damping_of(last - 1) * below
        low_a = lift * ea
        low_b = lift * eb
        land = mask[...].astype(jnp.float32)
        drive = 0.25 * land * (slope[0] * (top_a + low_a) + slope[1] * (top_b + low_b))
        for j in range(nz):
            late[j] = drive[j * size : (j + 1) * size, :]
        for j in range(top):
            late_copy(j).start()
        adj_out[0, last] = adj_out[0, last] + top_a
        adj_out[1, last] = adj_out[1, last] + top_b
        adj_out[0, last - 1] = adj_out[0, last - 1] + low_a
        adj_out[1, last - 1] = adj_out[1, last - 1] + low_b
        for j in range(top):
            late_copy(j).wait_send()

    gathered = part[:, own_rows, :]
    for o in range(1, nz):
        part_copy(o).wait_recv()
        gathered = gathered + part_in[o - 1]
    maps_out[0] = gathered[0]

    @pl.when(is_top)
    def _():
        maps_out[1] = gathered[1] + late[top]

    @pl.when(gz < top)
    def _():
        remote(late.at[0], late_in, late_sem.at[0, 0], late_sem.at[1, 0], (gx, gy, top)).wait_recv()
        maps_out[1] = gathered[1] + late_in[...]

    for bit in range(bits):
        for g in range(groups):
            half_copy(bit, g).wait_send()
    for t in range(tiles):

        @pl.when(tile != t)
        def _(t=t):
            tile_copy(t).wait_send()

    @pl.when(gz < top)
    def _():
        to_last.wait_send()

    for copy, sends in ring_sends:

        @pl.when(sends)
        def _(copy=copy):
            copy.wait_send()

    for o in range(1, nz):
        part_copy(o).wait_send()


def apply_twice(count, pixels, guess, visc, fric, base, slope, mask, counts):
    nx, ny, nz = counts
    tiles = nx * ny
    bits = nz.bit_length() - 1
    _, layers, rows, cols = guess.shape
    size = rows // nz
    f32 = jnp.float32
    groups = len(tile_spans(tiles))
    per_device = pixels[0].shape[0]
    cap = 2 * per_device // tiles
    chunk_rows = min(8, cap // 128)
    depth = chunk_rows * 128
    chunks = cap // depth
    flat = [value.reshape(per_device // 128, 128) for value in pixels]
    halves = [pltpu.VMEM((nz >> (bit + 1), tiles, 2, size, cols), f32) for bit in range(bits)]
    vmem = pl.BlockSpec(memory_space=pltpu.VMEM)
    dma = pltpu.SemaphoreType.DMA
    return pl.pallas_call(
        functools.partial(apply_kernel, counts),
        in_specs=[pl.BlockSpec(memory_space=pltpu.SMEM)] + [vmem] * 10,
        out_specs=(vmem, vmem),
        out_shape=(pltpu.VMEM(guess.shape, f32), pltpu.VMEM((2, size, cols), f32)),
        scratch_shapes=halves
        + halves
        + [
            pltpu.VMEM((6, tiles * chunks, chunk_rows, 128), f32),
            pltpu.VMEM((nz, tiles, 2, size, cols), f32),
            pltpu.VMEM((chunks, 4 * rows, depth), jnp.bfloat16),
            pltpu.VMEM((chunks, cols, depth), jnp.bfloat16),
            pltpu.VMEM((4 * rows, cols), f32),
            pltpu.VMEM((tiles, 2, size, cols), f32),
            pltpu.VMEM((2, size, cols), f32),
            pltpu.VMEM((nz, 2, size, cols), f32),
            pltpu.VMEM(guess.shape, f32),
            pltpu.VMEM((rows, 128), f32),
            pltpu.VMEM((rows, 128), f32),
            pltpu.VMEM((24, cols), f32),
            pltpu.VMEM((24, cols), f32),
            pltpu.VMEM((2, rows, 128), f32),
            pltpu.VMEM((2, rows, 128), f32),
            pltpu.VMEM((2, 24, cols), f32),
            pltpu.VMEM((2, 24, cols), f32),
            pltpu.VMEM((2, 24, 128), f32),
            pltpu.VMEM((2, 8, 128), f32),
            pltpu.VMEM((2, 2, rows, cols), f32),
            pltpu.VMEM((2, 2, rows, cols), f32),
            pltpu.VMEM((rows, cols), f32),
            pltpu.VMEM((2, rows, cols), f32),
            pltpu.VMEM((nz - 1, 2, size, cols), f32),
            pltpu.VMEM((size, 128), f32),
            pltpu.VMEM((size, 128), f32),
            pltpu.VMEM((16, cols), f32),
            pltpu.VMEM((16, cols), f32),
            pltpu.VMEM((nz, size, 128), f32),
            pltpu.VMEM((nz, size, 128), f32),
            pltpu.VMEM((16, cols), f32),
            pltpu.VMEM((16, cols), f32),
            pltpu.VMEM((16, 128), f32),
            pltpu.VMEM((8, 128), f32),
            pltpu.VMEM((nz, size, cols), f32),
            pltpu.VMEM((size, cols), f32),
            dma((2, bits, groups)),
            dma((2, tiles)),
            dma,
            dma((nz,)),
            dma((2, 2, 8)),
            dma((2,)),
            dma((2, nz - 1)),
            dma((6,)),
            dma((2 * nz + 4,)),
            dma((2, nz)),
        ],
        compiler_params=pltpu.CompilerParams(
            collective_id=0, has_side_effects=True, vmem_limit_bytes=56 * 2**20
        ),
        name="apply_twice",
    )(count, *flat, guess, visc, fric, base, slope, mask)


def body(
    adjoint_guess,
    viscosity,
    friction,
    base_velocity,
    surface_slope,
    ice_mask,
    pixel_misfit,
    pixel_look,
    pixel_tile,
    pixel_cell,
    pixel_count,
):
    sizes = tuple(lax.axis_size(name) for name in ("gx", "gy", "gz"))
    pixels = (pixel_misfit, pixel_look, pixel_tile[:, 0], pixel_cell)
    return apply_twice(
        pixel_count,
        pixels,
        adjoint_guess,
        viscosity,
        friction,
        base_velocity,
        surface_slope,
        ice_mask,
        sizes,
    )


def solution(mesh):
    return jax.shard_map(
        body,
        mesh=mesh,
        in_specs=(
            P(None, "gz", "gy", "gx"),
            P("gz", "gy", "gx"),
            P("gy", "gx"),
            P(None, "gy", "gx"),
            P(None, "gy", "gx"),
            P("gy", "gx"),
            P(("gx", "gy", "gz")),
            P(("gx", "gy", "gz")),
            P(("gx", "gy", "gz"), None),
            P(("gx", "gy", "gz")),
            P(("gx", "gy", "gz")),
        ),
        out_specs=(P(None, "gz", "gy", "gx"), P(None, ("gy", "gz"), "gx")),
        check_vma=False,
    )
```
